32 devices in a mesh: seq: 8 (over y, x, core), head: 4 (over z).
Axes of the slice: x: 2, y: 2, z: 4, core: 2. Of those that a mesh axis runs over, the one named last changes fastest.
Arguments:
- frames: bfloat16 [8192, 1024], P(('seq', 'head')), may hold values from -6 to 6
- cotangent: bfloat16 [8192, 1024], P(('seq', 'head')), may hold values from -6 to 6
- norm_gain: float32 [1024], replicated, may hold values from 0.25 to 1.75
- w_qkv: bfloat16 [3, 1024, 1024], replicated
- w_out: bfloat16 [1024, 1024], replicated, may hold values from -0.1875 to 0.1875
Outputs:
- output: bfloat16 [8192, 1024], P(('seq', 'head'))
- grad_frames: bfloat16 [8192, 1024], P(('seq', 'head'))
- grad_qkv: float32 [3, 1024, 1024], P(None, 'seq', 'head')
- grad_out: float32 [1024, 1024], P('seq', 'head')
The draws below stay inside these ranges and needn't reach their ends.
All inputs are finite; a program needn't handle non-finite values.
Results may differ from the reference program's by a relative error of at most 0.015.
Values may be sent and summed in bfloat16 or wider, within the bound.
A program may use at most 128 MiB of HBM per device.

```python
import jax
import jax.numpy as jnp
from jax import lax

D = 1024
HEAD_SIZE = 128
WINDOW = 128
FRAMES = 8192


def draw_w_qkv(key, part):
    base = jax.random.normal(key, (3, D, D), jnp.float32) * D ** (-0.5)
    return base.astype(jnp.bfloat16)


def spiked(array, own_key, source, target, parts, factor):
    def block_of(position):
        return (jnp.arange(array.shape[position]) // (array.shape[position] // parts)).reshape((-1,) + (1,) * (array.ndim - 1 - position))

    one_side = jax.random.permutation(own_key, parts)[block_of(target)]
    second = (block_of(target) + parts // 2) % parts
    return jnp.where((block_of(source) == one_side) | (block_of(source) == second), factor * array, array)


def levels(own_key, dims, pieces, low, top_value):
    level = 1.0
    for position, blocks in pieces:
        draws = jax.random.uniform(jax.random.fold_in(jax.random.fold_in(own_key, 6), position), (blocks,), jnp.float32, low / len(pieces), top_value / len(pieces))
        level = level * jnp.repeat(jnp.exp(draws), dims[position] // blocks).reshape((-1,) + (1,) * (len(dims) - 1 - position))
    return level


def scatter_about(key, extent, deviation, reach, cuts=(), kind=jnp.bfloat16):
    result = deviation * jax.random.normal(key, extent, jnp.float32)
    if cuts:
        result = result * levels(key, extent, cuts, -0.22, 0.18)
    return jnp.clip(result, -reach, reach).astype(kind)


def gaussian_with(own_key, dims, spread, reach, pieces, heavy, kind=jnp.bfloat16):
    entries = spread * jax.random.normal(own_key, dims, jnp.float32)
    if pieces:
        entries = entries * levels(own_key, dims, pieces, -0.22, 0.18)
    return jnp.clip(spiked(entries, jax.random.fold_in(own_key, 3), *heavy), -reach, reach).astype(kind)


def setup_inputs(seed: int = 0) -> dict:
    splits = jax.random.split(jax.random.key(seed), 6)
    return {
        "frames": scatter_about(splits[0], (FRAMES, D), 1.0, 6.0, ((0, 32),)),
        "cotangent": gaussian_with(splits[1], (FRAMES, D), 1.0, 6.0, ((0, 32),), (0, 1, 32, 2.75)),
        "norm_gain": jnp.clip(1.0 + 0.15 * jax.random.normal(splits[2], (D,), jnp.float32), 0.25, 1.75),
        "w_qkv": draw_w_qkv(jax.random.fold_in(splits[5], 71), 0),
        "w_out": scatter_about(splits[4], (D, D), D ** -0.5, 0.1875),
    }


EPSILON = 1e-05
MASKED = -1e+30

def layer_norm(values, norm_gain):
    average = lax.optimization_barrier(jnp.mean(values, axis=-1, keepdims=True))
    centered = values - average
    variance = lax.optimization_barrier(jnp.mean(centered * centered, axis=-1, keepdims=True))
    return centered * lax.rsqrt(variance + EPSILON) * norm_gain

def norm_grad(frames, norm_gain, upstream):
    _, pullback = jax.vjp(lambda v: layer_norm(v, norm_gain), frames.astype(jnp.float32))
    return pullback(upstream.astype(jnp.float32))[0]

def attention(query_rows, key_rows, value_rows, offset, frame_total):
    length, channels = query_rows.shape
    head_count = channels // HEAD_SIZE
    block_rows = min(length, 512)
    block_count = length // block_rows
    key_span = block_rows + 2 * WINDOW
    score_scale = HEAD_SIZE ** (-0.5)

    def one_block(block_index):
        anchor = block_index * block_rows
        query_part = lax.dynamic_slice_in_dim(query_rows, anchor, block_rows, 0).reshape(block_rows, head_count, HEAD_SIZE)
        key_part = lax.dynamic_slice_in_dim(key_rows, anchor, key_span, 0).reshape(key_span, head_count, HEAD_SIZE)
        value_part = lax.dynamic_slice_in_dim(value_rows, anchor, key_span, 0).reshape(key_span, head_count, HEAD_SIZE)
        query_pos = offset + anchor + jnp.arange(block_rows, dtype=jnp.int32)
        key_pos = offset + anchor - WINDOW + jnp.arange(key_span, dtype=jnp.int32)
        distance = query_pos[:, None] - key_pos[None, :]
        allowed = (jnp.abs(distance) <= WINDOW) & (key_pos >= 0)[None, :] & (key_pos < frame_total)[None, :]
        scores = jnp.einsum('qhe,khe->hqk', query_part, key_part, precision=lax.Precision.HIGHEST) * score_scale
        scores = jnp.where(allowed[None], scores, MASKED)
        row_max = lax.stop_gradient(lax.optimization_barrier(jnp.max(scores, axis=-1, keepdims=True)))
        weights = jnp.exp(scores - row_max)
        weights = weights / lax.optimization_barrier(jnp.sum(weights, axis=-1, keepdims=True))
        combined = jnp.einsum('hqk,khe->qhe', weights, value_part, precision=lax.Precision.HIGHEST)
        return combined.reshape(block_rows, channels)
    results = lax.map(jax.checkpoint(one_block), jnp.arange(block_count, dtype=jnp.int32))
    return results.reshape(length, channels)

def attention_grad(query_rows, key_rows, value_rows, offset, frame_total, upstream):
    _, pullback = jax.vjp(lambda a, b, c: attention(a, b, c, offset, frame_total), query_rows, key_rows, value_rows)
    return pullback(upstream.astype(jnp.float32))

def reference(frames, cotangent, norm_gain, w_qkv, w_out):
    frame_total = frames.shape[0]
    grad_scale = frame_total ** (-0.5)
    normed = layer_norm(frames.astype(jnp.float32), norm_gain).astype(jnp.bfloat16)
    projected = jnp.stack([jnp.dot(normed, w_qkv[member], preferred_element_type=jnp.float32) for member in range(3)]).astype(jnp.bfloat16)
    query_rows = projected[0].astype(jnp.float32)
    key_rows = jnp.pad(projected[1].astype(jnp.float32), ((WINDOW, WINDOW), (0, 0)))
    value_rows = jnp.pad(projected[2].astype(jnp.float32), ((WINDOW, WINDOW), (0, 0)))
    anchor = jnp.zeros((), jnp.int32)
    attended = attention(query_rows, key_rows, value_rows, anchor, frame_total).astype(jnp.bfloat16)
    output = (frames.astype(jnp.float32) + jnp.dot(attended, w_out, preferred_element_type=jnp.float32)).astype(jnp.bfloat16)
    grad_attended = jnp.dot(cotangent, w_out.T, preferred_element_type=jnp.float32).astype(jnp.bfloat16)
    grad_out = jnp.dot(attended.T, cotangent, preferred_element_type=jnp.float32) * grad_scale
    grad_query, grad_keys, grad_values = attention_grad(query_rows, key_rows, value_rows, anchor, frame_total, grad_attended)
    grad_proj = jnp.stack([grad_query, grad_keys[WINDOW:WINDOW + frame_total], grad_values[WINDOW:WINDOW + frame_total]]).astype(jnp.bfloat16)
    grad_sum = jnp.dot(grad_proj[0], w_qkv[0].T, preferred_element_type=jnp.float32)
    grad_sum = grad_sum + jnp.dot(grad_proj[1], w_qkv[1].T, preferred_element_type=jnp.float32)
    grad_sum = grad_sum + jnp.dot(grad_proj[2], w_qkv[2].T, preferred_element_type=jnp.float32)
    grad_normed = grad_sum.astype(jnp.bfloat16)
    grad_frames = (cotangent.astype(jnp.float32) + norm_grad(frames, norm_gain, grad_normed)).astype(jnp.bfloat16)
    grad_qkv = jnp.stack([jnp.dot(normed.T, grad_proj[member], preferred_element_type=jnp.float32) for member in range(3)]) * grad_scale
    return (output, grad_frames, grad_qkv, grad_out)
```

```python
import functools

import jax
import jax.numpy as jnp
from jax import lax
from jax.experimental import pallas as pl
from jax.experimental.pallas import tpu as pltpu
from jax.sharding import PartitionSpec as P

HEAD_SIZE = 128
WINDOW = 128

EPSILON = 1e-05
MASKED = -1e30
AXES = ("seq", "head")


def dot(a, b, contract):
    return lax.dot_general(a, b, (contract, ((), ())), preferred_element_type=jnp.float32)


def bits_of(size):
    return list(range(size.bit_length() - 1))


def block_kernel(
    sizes,
    frames, cotangent, gain, w_qkv_hbm, w_out_hbm,
    output, grad_frames, grad_qkv, grad_out,
    w_qkv, w_out, normed, normed_t, query, key, value, upstream, attended, attended_t,
    grad_query, grad_pair, shares, edge_out, edge_in, grad_normed, halo, mail, got, held, landed, last,
    weight_sem, halo_send, halo_recv, edge_send, edge_recv,
    core_send, core_recv, stage_send, stage_recv, last_send, last_recv,
):
    seq_size, head_size = sizes
    devices = seq_size * head_size
    length, channels = frames.shape
    outer, part_rows, tile_cols = held.shape[2], held.shape[4], held.shape[5]
    tile_rows = 2 * part_rows
    bits = bits_of(outer)
    orders = (bits, bits[::-1])
    levels = len(bits)
    seq, head = lax.axis_index("seq"), lax.axis_index("head")
    core, row_block = seq % 2, seq // 2
    position = seq * head_size + head
    bf16, f32 = jnp.bfloat16, jnp.float32
    strip = min(256, channels)

    def neighbour(step):
        there = (position + step + devices) % devices
        return (there // head_size, there % head_size)

    def bit_at(bit):
        return (row_block // 2**bit) % 2

    def partner(bit):
        return (2 * (row_block + (1 - 2 * bit_at(bit)) * 2**bit) + core, head)

    def along(step):
        return (seq, (head + step) % head_size)

    weights = [pltpu.make_async_copy(w_out_hbm, w_out, weight_sem.at[3])]
    for which in range(3):
        weights.append(
            pltpu.make_async_copy(w_qkv_hbm.at[which], w_qkv.at[which], weight_sem.at[which])
        )
    for one in weights:
        one.start()

    other_core = (2 * row_block + 1 - core, head)
    greeted = [other_core] + [partner(bit) for bit in bits]
    greeted += [along(step) for step in range(1, head_size)] + [neighbour(1), neighbour(-1)]
    barrier = pltpu.get_barrier_semaphore()
    for device in greeted:
        pl.semaphore_signal(barrier, inc=1, device_id=device, device_id_type=pl.DeviceIdType.MESH)
    pl.semaphore_wait(barrier, len(greeted))

    def halo_copy(side):
        rows = pl.ds(length - WINDOW, WINDOW) if side == 0 else pl.ds(0, WINDOW)
        return pltpu.make_async_remote_copy(
            src_ref=frames.at[rows],
            dst_ref=halo.at[side],
            send_sem=halo_send.at[side],
            recv_sem=halo_recv.at[side],
            device_id=neighbour(1 if side == 0 else -1),
            device_id_type=pl.DeviceIdType.MESH,
        )

    halo_copy(0).start()
    halo_copy(1).start()

    def standardise(values):
        average = jnp.mean(values, axis=-1, keepdims=True)
        centered = values - average
        variance = jnp.mean(centered * centered, axis=-1, keepdims=True)
        inverse = lax.rsqrt(variance + EPSILON)
        return centered * inverse, inverse

    few = 64

    def norm_rows(source, target_row, rows):
        def one(step, carry):
            values = source[pl.ds(pl.multiple_of(step * few, few), few), :].astype(f32)
            rounded = (standardise(values)[0] * gain[...]).astype(bf16)
            normed[pl.ds(pl.multiple_of(target_row + step * few, few), few), :] = rounded
            return carry

        lax.fori_loop(0, rows // few, one, 0)

    def multiply_into(target, rows, left, weight, side):
        for start in range(0, channels, strip):
            cols = slice(start, start + strip)
            other = weight[:, cols] if side == 0 else weight[cols, :]
            target[rows, cols] = dot(left, other, ((1,), (side,))).astype(target.dtype)

    norm_rows(frames, WINDOW, length)
    own = slice(WINDOW, WINDOW + length)

    piece = min(128, tile_rows)

    def store_turned(target, first, cols, turned):
        for start in range(0, 128, piece):
            block = (first + start) // tile_rows
            down = (block // 2) * tile_rows + (first + start) % tile_rows
            target[block % 2, pl.ds(pl.multiple_of(down, piece), piece), cols] = turned[start : start + piece]

    def turn(first, last):
        for start in range(first, last, 128):
            for col in range(0, channels, 128):
                tile = normed[start : start + 128, col : col + 128]
                store_turned(normed_t, col, slice(start, start + 128), tile.astype(f32).T.astype(bf16))

    turn(WINDOW, WINDOW + length)
    weights[0].wait()
    everything = slice(0, length)
    multiply_into(upstream, everything, cotangent[...], w_out, 1)
    for which, target, rows in ((0, query, everything), (1, key, own), (2, value, own)):
        weights[1 + which].wait()
        multiply_into(target, rows, normed[own, :], w_qkv.at[which], 0)
    for side in range(2):
        halo_copy(side).wait()
        start = side * (length + WINDOW)
        norm_rows(halo.at[side], start, WINDOW)
    for side in range(2):
        start = side * (length + WINDOW)
        rows = slice(start, start + WINDOW)
        multiply_into(key, rows, normed[rows, :], w_qkv.at[1], 0)
        multiply_into(value, rows, normed[rows, :], w_qkv.at[2], 0)

    wide = 2 * HEAD_SIZE
    pairs = channels // wide

    def edge_copy(side):
        return pltpu.make_async_remote_copy(
            src_ref=edge_out.at[side],
            dst_ref=edge_in.at[side],
            send_sem=edge_send.at[side],
            recv_sem=edge_recv.at[side],
            device_id=neighbour(-1 if side == 0 else 1),
            device_id_type=pl.DeviceIdType.MESH,
        )

    blocks = length // WINDOW
    span = 3 * WINDOW
    score_scale = HEAD_SIZE ** (-0.5)
    row = lax.broadcasted_iota(jnp.int32, (WINDOW, span), 0)
    col = lax.broadcasted_iota(jnp.int32, (WINDOW, span), 1)
    near = (col >= row) & (col <= row + 2 * WINDOW)

    def forward(pair, carry):
        for head in range(wide // HEAD_SIZE):
            lane = pl.multiple_of(pair * wide + head * HEAD_SIZE, HEAD_SIZE)
            lanes = pl.ds(lane, HEAD_SIZE)
            for block in range(blocks):
                rows = slice(block * WINDOW, (block + 1) * WINDOW)
                keys = slice(block * WINDOW, block * WINDOW + span)
                q, k, v = query[rows, lanes], key[keys, lanes], value[keys, lanes]
                frame = position * length + (block - 1) * WINDOW + col
                allowed = near & (frame >= 0) & (frame < devices * length)
                scores = jnp.where(allowed, dot(q, k, ((1,), (1,))) * score_scale, MASKED)
                share = jnp.exp(scores - jnp.max(scores, axis=-1, keepdims=True))
                share = (share * (1.0 / jnp.sum(share, axis=-1, keepdims=True))).astype(bf16)
                shares[pair * (wide // HEAD_SIZE) + head, block] = share
                mixed = dot(share, v, ((1,), (0,)))
                attended[rows, lanes] = mixed.astype(bf16)
                store_turned(attended_t, lane, rows, mixed.T.astype(bf16))
        return carry

    def backward(pair, carry):
        for head in range(wide // HEAD_SIZE):
            lane = pl.multiple_of(pair * wide + head * HEAD_SIZE, HEAD_SIZE)
            lanes = pl.ds(lane, HEAD_SIZE)
            key_grads = [None] * (blocks + 2)
            value_grads = [None] * (blocks + 2)
            for block in range(blocks):
                rows = slice(block * WINDOW, (block + 1) * WINDOW)
                keys = slice(block * WINDOW, block * WINDOW + span)
                q, k, v, up = query[rows, lanes], key[keys, lanes], value[keys, lanes], upstream[rows, lanes]
                rounded = shares[pair * (wide // HEAD_SIZE) + head, block]
                share = rounded.astype(f32)
                grad = dot(up, v, ((1,), (1,)))
                centre = jnp.sum(share * grad, axis=-1, keepdims=True)
                grad = (share * (grad - centre) * score_scale).astype(bf16)
                grad_query[rows, lanes] = dot(grad, k, ((1,), (0,))).astype(bf16)
                key_grad = dot(grad, q, ((0,), (0,)))
                value_grad = dot(rounded, up, ((0,), (0,)))
                for part in range(3):
                    piece = slice(part * WINDOW, (part + 1) * WINDOW)
                    for sums, term in ((key_grads, key_grad[piece]), (value_grads, value_grad[piece])):
                        before = sums[block + part]
                        sums[block + part] = term if before is None else before + term
            for which, sums in enumerate((key_grads, value_grads)):
                for block in range(blocks + 2):
                    rows = slice(block * WINDOW, (block + 1) * WINDOW)
                    grad_pair[which, rows, lanes] = sums[block].astype(bf16)
        return carry

    def spot(lane, block):
        return sum(((block >> bit) & 1) * (outer >> (step + 1)) for step, bit in enumerate(orders[lane]))

    def base(lane, stage):
        total = 0
        for step in range(stage):
            total = total + bit_at(orders[lane][step]) * (outer >> (step + 1))
        return total

    def landing(stage):
        return outer - (outer >> stage)

    def leaving(lane, stage):
        return base(lane, stage) + (1 - bit_at(orders[lane][stage])) * (outer >> (stage + 1))

    def core_copy(chunk):
        return pltpu.make_async_remote_copy(
            src_ref=mail.at[chunk],
            dst_ref=got.at[chunk],
            send_sem=core_send.at[chunk],
            recv_sem=core_recv.at[chunk],
            device_id=other_core,
            device_id_type=pl.DeviceIdType.MESH,
        )

    def stage_copy(chunk, lane, stage):
        half = outer >> (stage + 1)
        return pltpu.make_async_remote_copy(
            src_ref=held.at[chunk, lane, pl.ds(leaving(lane, stage), half)],
            dst_ref=landed.at[chunk, lane, pl.ds(landing(stage), half)],
            send_sem=stage_send.at[chunk, lane, stage],
            recv_sem=stage_recv.at[chunk, lane, stage],
            device_id=partner(orders[lane][stage]),
            device_id_type=pl.DeviceIdType.MESH,
        )

    def last_copy(chunk, lane, step):
        return pltpu.make_async_remote_copy(
            src_ref=held.at[chunk, lane, base(lane, levels), (head + step) % head_size],
            dst_ref=last.at[chunk, lane, step - 1],
            send_sem=last_send.at[chunk, lane, step - 1],
            recv_sem=last_recv.at[chunk, lane, step - 1],
            device_id=along(step),
            device_id_type=pl.DeviceIdType.MESH,
        )

    def gathered(chunk, lane, stage, where, col):
        total = held[chunk, lane, where, col].astype(f32) + got[chunk, lane, where, col].astype(f32)
        for step in range(stage):
            total = total + landed[chunk, lane, landing(step) + where - base(lane, step + 1), col].astype(f32)
        return total

    def send_on(chunk, lane, stage):
        if stage == 0:
            if lane == 0:
                core_copy(chunk).wait()
        else:
            stage_copy(chunk, lane, stage - 1).wait()
        if stage < levels:
            half = outer >> (stage + 1)
            start = leaving(lane, stage)

            def add(step, carry):
                where, col = start + step // head_size, step % head_size
                held[chunk, lane, where, col] = gathered(chunk, lane, stage, where, col).astype(bf16)
                return carry

            lax.fori_loop(0, half * head_size, add, 0)
            stage_copy(chunk, lane, stage).start()
            return
        where = base(lane, levels)
        for step in range(1, head_size):
            col = (head + step) % head_size
            held[chunk, lane, where, col] = gathered(chunk, lane, stage, where, col).astype(bf16)
            last_copy(chunk, lane, step).start()

    def advance(chunk, stage):
        for lane in range(2):
            send_on(chunk, lane, stage)

    def finish(chunk):
        for lane in range(2):
            total = gathered(chunk, lane, levels, base(lane, levels), head)
            for step in range(1, head_size):
                last_copy(chunk, lane, step).wait()
                total = total + last[chunk, lane, step - 1].astype(f32)
            rows = slice(lane * part_rows, (lane + 1) * part_rows)
            if chunk == 0:
                grad_out[rows, :] = total
            else:
                grad_qkv[chunk - 1, rows, :] = total

    def products(chunk, target, parity, left, right, depth):
        def one(col, carry):
            cols = pl.ds(pl.multiple_of(col * tile_cols, tile_cols), tile_cols)
            product = dot(left[parity, :, depth], right[:, cols], ((1,), (0,))).astype(bf16)
            for block in range(outer):
                for lane in range(2):
                    start = block * tile_rows + lane * part_rows
                    target[chunk, lane, spot(lane, block), col] = product[start : start + part_rows]
            return carry

        lax.fori_loop(0, head_size, one, 0)

    def launch(chunk, left, right, depth):
        products(chunk, mail, 1 - core, left, right, depth)
        core_copy(chunk).start()
        products(chunk, held, core, left, right, depth)

    def pair_back(rows, cols):
        term = dot(grad_pair[0, rows, :], w_qkv[1, cols, :], ((1,), (1,)))
        return term + dot(grad_pair[1, rows, :], w_qkv[2, cols, :], ((1,), (1,)))

    def norm_back(step, carry):
        rows = pl.ds(pl.multiple_of(step * few, few), few)
        unit, inverse = standardise(frames[rows, :].astype(f32))
        grad = grad_normed[rows, :].astype(bf16).astype(f32) * gain[...]
        average = jnp.mean(grad, axis=-1, keepdims=True)
        along_unit = jnp.mean(grad * unit, axis=-1, keepdims=True)
        grad = inverse * (grad - average - unit * along_unit)
        grad_frames[rows, :] = (cotangent[rows, :].astype(f32) + grad).astype(bf16)
        return carry

    whole = slice(0, 2 * WINDOW + length)
    lax.fori_loop(0, pairs, forward, 0)
    launch(0, attended_t, cotangent, everything)
    lax.fori_loop(0, 1, backward, 0)
    advance(0, 0)
    lax.fori_loop(1, pairs, backward, 0)
    turn(0, WINDOW)
    turn(WINDOW + length, 2 * WINDOW + length)
    launch(3, normed_t, grad_pair.at[1], whole)
    advance(0, 1)
    advance(3, 0)
    launch(2, normed_t, grad_pair.at[0], whole)
    advance(0, 2)
    advance(2, 0)
    launch(1, normed_t, grad_query, own)
    advance(1, 0)
    advance(3, 1)
    for side in range(2):
        start = side * (length + WINDOW)
        for strip_start in range(0, channels, strip):
            cols = slice(strip_start, strip_start + strip)
            edge_out[side, :, cols] = pair_back(slice(start, start + WINDOW), cols).astype(bf16)
        edge_copy(side).start()
    advance(3, 2)
    for start in range(0, channels, strip):
        cols = slice(start, start + strip)
        mixed = dot(attended[...], w_out[:, cols], ((1,), (0,)))
        output[:, cols] = (frames[:, cols].astype(f32) + mixed).astype(bf16)
    advance(2, 1)
    for start in range(0, channels, strip):
        cols = slice(start, start + strip)
        grad_normed[:, cols] = pair_back(own, cols) + dot(grad_query[...], w_qkv[0, cols, :], ((1,), (1,)))
    advance(1, 1)
    advance(2, 2)
    finish(0)
    edge_copy(0).wait()
    edge_copy(1).wait()
    grad_normed[:WINDOW, :] += edge_in[1].astype(f32)
    grad_normed[length - WINDOW :, :] += edge_in[0].astype(f32)
    lax.fori_loop(0, length // few, norm_back, 0)
    advance(1, 2)
    finish(3)
    finish(2)
    finish(1)


def deliver_kernel(scale, output, grad_frames, grad_qkv, grad_out, *targets):
    targets[0][...] = output[...]
    targets[1][...] = grad_frames[...]
    targets[2][...] = grad_qkv[...] * scale
    targets[3][...] = grad_out[...] * scale


def shards(frames, cotangent, norm_gain, w_qkv, w_out):
    length, channels = frames.shape
    seq_size, head_size = lax.axis_size("seq"), lax.axis_size("head")
    devices = seq_size * head_size
    bordered = length + 2 * WINDOW
    tile_rows, tile_cols = channels // seq_size, channels // head_size
    chunks, outer = 4, seq_size // 2
    levels = len(bits_of(outer))
    part = (tile_rows // 2, tile_cols)
    bf16, f32 = jnp.bfloat16, jnp.float32
    vmem, anywhere = pl.BlockSpec(memory_space=pltpu.VMEM), pl.BlockSpec(memory_space=pl.ANY)
    dma = pltpu.SemaphoreType.DMA
    shapes = [
        jax.ShapeDtypeStruct((length, channels), bf16),
        jax.ShapeDtypeStruct((length, channels), bf16),
        jax.ShapeDtypeStruct((3, tile_rows, tile_cols), f32),
        jax.ShapeDtypeStruct((tile_rows, tile_cols), f32),
    ]
    results = pl.pallas_call(
        functools.partial(block_kernel, (seq_size, head_size)),
        out_shape=shapes,
        in_specs=[vmem, vmem, vmem, anywhere, anywhere],
        out_specs=[vmem] * 4,
        scratch_shapes=[
            pltpu.VMEM((3, channels, channels), bf16),
            pltpu.VMEM((channels, channels), bf16),
            pltpu.VMEM((bordered, channels), bf16),
            pltpu.VMEM((2, channels // 2, bordered), bf16),
            pltpu.VMEM((length, channels), bf16),
            pltpu.VMEM((bordered, channels), bf16),
            pltpu.VMEM((bordered, channels), bf16),
            pltpu.VMEM((length, channels), bf16),
            pltpu.VMEM((length, channels), bf16),
            pltpu.VMEM((2, channels // 2, length), bf16),
            pltpu.VMEM((length, channels), bf16),
            pltpu.VMEM((2, bordered, channels), bf16),
            pltpu.VMEM((channels // HEAD_SIZE, length // WINDOW, WINDOW, 3 * WINDOW), bf16),
            pltpu.VMEM((2, WINDOW, channels), bf16),
            pltpu.VMEM((2, WINDOW, channels), bf16),
            pltpu.VMEM((length, channels), f32),
            pltpu.VMEM((2, WINDOW, channels), bf16),
            pltpu.VMEM((chunks, 2, outer, head_size, *part), bf16),
            pltpu.VMEM((chunks, 2, outer, head_size, *part), bf16),
            pltpu.VMEM((chunks, 2, outer, head_size, *part), bf16),
            pltpu.VMEM((chunks, 2, outer - 1, head_size, *part), bf16),
            pltpu.VMEM((chunks, 2, head_size - 1, *part), bf16),
            dma((4,)),
            dma((2,)),
            dma((2,)),
            dma((2,)),
            dma((2,)),
            dma((chunks,)),
            dma((chunks,)),
            dma((chunks, 2, levels)),
            dma((chunks, 2, levels)),
            dma((chunks, 2, head_size - 1)),
            dma((chunks, 2, head_size - 1)),
        ],
        compiler_params=pltpu.CompilerParams(
            collective_id=0, has_side_effects=True, vmem_limit_bytes=60 * 2**20
        ),
        name="block",
    )(frames, cotangent, norm_gain.reshape(1, channels), w_qkv, w_out)
    return tuple(
        pl.pallas_call(
            functools.partial(deliver_kernel, (devices * length) ** (-0.5)),
            out_shape=shapes,
            in_specs=[vmem] * 4,
            out_specs=[vmem] * 4,
            name="deliver",
        )(*results)
    )


def solution(mesh):
    in_specs = (P(("seq", "head"), None), P(("seq", "head"), None), P(), P(), P())
    out_specs = (
        P(("seq", "head"), None),
        P(("seq", "head"), None),
        P(None, "seq", "head"),
        P("seq", "head"),
    )
    return jax.shard_map(shards, mesh=mesh, in_specs=in_specs, out_specs=out_specs, check_vma=False)
```

```python
import functools

import jax
import jax.numpy as jnp
from jax import lax
from jax.experimental import pallas as pl
from jax.experimental.pallas import tpu as pltpu
from jax.sharding import PartitionSpec as P

HEAD_SIZE = 128
WINDOW = 128

EPSILON = 1e-05
MASKED = -1e30
AXES = ("seq", "head")


def dot(a, b, contract):
    return lax.dot_general(a, b, (contract, ((), ())), preferred_element_type=jnp.float32)


def bits_of(size):
    return list(range(size.bit_length() - 1))


def block_kernel(
    sizes,
    frames, cotangent, gain, w_qkv_hbm, w_out_hbm,
    output, grad_frames, grad_qkv, grad_out,
    w_qkv, w_out, normed, normed_t, query, key, value, upstream, attended, attended_t,
    grad_query, grad_pair, edge_out, edge_in, grad_normed, halo, halo_normed,
    mail, got, held, landed, last, mail_out, got_out, held_out, landed_out, last_out,
    weight_sem, halo_send, halo_recv, edge_send, edge_recv,
    core_send, core_recv, stage_send, stage_recv, last_send, last_recv, last_send_out, last_recv_out,
):
    seq_size, head_size = sizes
    devices = seq_size * head_size
    length, channels = frames.shape
    outer, part_rows, tile_cols = held_out.shape[1], held_out.shape[3], held_out.shape[4]
    tile_rows = 2 * part_rows
    bits = bits_of(outer)
    orders = (bits, bits[::-1])
    levels = len(bits)
    seq, head = lax.axis_index("seq"), lax.axis_index("head")
    core, row_block = seq % 2, seq // 2
    position = seq * head_size + head
    bf16, f32 = jnp.bfloat16, jnp.float32
    strip = min(256, channels)

    def neighbour(step):
        there = (position + step + devices) % devices
        return (there // head_size, there % head_size)

    def bit_at(bit):
        return (row_block // 2**bit) % 2

    def partner(bit):
        return (2 * (row_block + (1 - 2 * bit_at(bit)) * 2**bit) + core, head)

    def along(step):
        return (seq, (head + step) % head_size)

    wide = 2 * HEAD_SIZE
    pairs = channels // wide
    heads_each = tile_cols // HEAD_SIZE

    for slot in range(2 * pairs):
        real = slot // 2 + (slot % 2) * pairs
        there, here = pl.ds(real * HEAD_SIZE, HEAD_SIZE), pl.ds(slot * HEAD_SIZE, HEAD_SIZE)
        pltpu.make_async_copy(w_out_hbm.at[there], w_out.at[here], weight_sem.at[3]).start()
    for which in range(3):
        for slot in range(2 * pairs):
            real = slot // 2 + (slot % 2) * pairs
            there, here = pl.ds(real * HEAD_SIZE, HEAD_SIZE), pl.ds(slot * HEAD_SIZE, HEAD_SIZE)
            pltpu.make_async_copy(
                w_qkv_hbm.at[which, :, there], w_qkv.at[which, :, here], weight_sem.at[which]
            ).start()

    def weight_wait(which):
        if which == 3:
            pltpu.make_async_copy(w_out_hbm, w_out, weight_sem.at[3]).wait()
        else:
            pltpu.make_async_copy(w_qkv_hbm.at[which], w_qkv.at[which], weight_sem.at[which]).wait()

    other_core = (2 * row_block + 1 - core, head)
    greeted = [other_core] + [partner(bit) for bit in bits]
    greeted += [along(step) for step in range(1, head_size)] + [neighbour(1), neighbour(-1)]
    barrier = pltpu.get_barrier_semaphore()
    for device in greeted:
        pl.semaphore_signal(barrier, inc=1, device_id=device, device_id_type=pl.DeviceIdType.MESH)
    pl.semaphore_wait(barrier, len(greeted))

    def halo_copy(side):
        rows = pl.ds(length - WINDOW, WINDOW) if side == 0 else pl.ds(0, WINDOW)
        return pltpu.make_async_remote_copy(
            src_ref=frames.at[rows],
            dst_ref=halo.at[side],
            send_sem=halo_send.at[side],
            recv_sem=halo_recv.at[side],
            device_id=neighbour(1 if side == 0 else -1),
            device_id_type=pl.DeviceIdType.MESH,
        )

    halo_copy(0).start()
    halo_copy(1).start()

    def standardise(values):
        average = jnp.mean(values, axis=-1, keepdims=True)
        centered = values - average
        variance = jnp.mean(centered * centered, axis=-1, keepdims=True)
        inverse = lax.rsqrt(variance + EPSILON)
        return centered * inverse, inverse

    few = 64

    def norm_rows(source, target, target_row, rows):
        def one(step, carry):
            values = source[pl.ds(pl.multiple_of(step * few, few), few), :].astype(f32)
            rounded = (standardise(values)[0] * gain[...]).astype(bf16)
            target[pl.ds(pl.multiple_of(target_row + step * few, few), few), :] = rounded
            return carry

        lax.fori_loop(0, rows // few, one, 0)

    def multiply_into(target, rows, left, weight, side):
        for start in range(0, channels, strip):
            cols = slice(start, start + strip)
            other = weight[:, cols] if side == 0 else weight[cols, :]
            target[rows, cols] = dot(left, other, ((1,), (side,))).astype(target.dtype)

    norm_rows(frames, normed, 0, length)
    own = slice(WINDOW, WINDOW + length)

    piece = min(128, tile_rows)

    def store_turned(target, first, cols, turned):
        for start in range(0, 128, piece):
            block = (first + start) // tile_rows
            down = (block // 2) * tile_rows + (first + start) % tile_rows
            target[block % 2, pl.ds(pl.multiple_of(down, piece), piece), cols] = turned[start : start + piece]

    def turn(source, row, place, rows):
        for start in range(0, rows, 128):
            for col in range(0, channels, 128):
                tile = source[row + start : row + start + 128, col : col + 128]
                cols = slice(place + start, place + start + 128)
                store_turned(normed_t, col, cols, tile.astype(f32).T.astype(bf16))

    turn(normed, 0, WINDOW, length)
    weight_wait(3)
    everything = slice(0, length)
    multiply_into(upstream, everything, cotangent[...], w_out, 1)
    for which, target, rows in ((0, query, everything), (1, key, own), (2, value, own)):
        weight_wait(which)
        multiply_into(target, rows, normed[...], w_qkv.at[which], 0)
    for side in range(2):
        halo_copy(side).wait()
        norm_rows(halo.at[side], halo_normed, side * WINDOW, WINDOW)
    for which, target in ((1, key), (2, value)):
        for start in range(0, channels, strip):
            cols = slice(start, start + strip)
            both = dot(halo_normed[...], w_qkv[which, :, cols], ((1,), (0,))).astype(bf16)
            target[:WINDOW, cols] = both[:WINDOW]
            target[WINDOW + length :, cols] = both[WINDOW:]
    turn(halo_normed, 0, 0, WINDOW)
    turn(halo_normed, WINDOW, WINDOW + length, WINDOW)

    def edge_copy(side):
        return pltpu.make_async_remote_copy(
            src_ref=edge_out.at[side],
            dst_ref=edge_in.at[side],
            send_sem=edge_send.at[side],
            recv_sem=edge_recv.at[side],
            device_id=neighbour(-1 if side == 0 else 1),
            device_id_type=pl.DeviceIdType.MESH,
        )

    blocks = length // WINDOW
    span = 3 * WINDOW
    score_scale = HEAD_SIZE ** (-0.5)
    row = lax.broadcasted_iota(jnp.int32, (WINDOW, span), 0)
    col = lax.broadcasted_iota(jnp.int32, (WINDOW, span), 1)
    near = (col >= row) & (col <= row + 2 * WINDOW)

    def attend(pair):
        for member in range(2):
            lane = pl.multiple_of(pair * wide + member * HEAD_SIZE, HEAD_SIZE)
            lanes = pl.ds(lane, HEAD_SIZE)
            real = (pair + member * pairs) * HEAD_SIZE
            key_grads = [None] * (blocks + 2)
            value_grads = [None] * (blocks + 2)
            for block in range(blocks):
                rows = slice(block * WINDOW, (block + 1) * WINDOW)
                keys = slice(block * WINDOW, block * WINDOW + span)
                q, k, v, up = query[rows, lanes], key[keys, lanes], value[keys, lanes], upstream[rows, lanes]
                frame = position * length + (block - 1) * WINDOW + col
                allowed = near & (frame >= 0) & (frame < devices * length)
                scores = jnp.where(allowed, dot(q, k, ((1,), (1,))) * score_scale, MASKED)
                share = jnp.exp(scores - jnp.max(scores, axis=-1, keepdims=True))
                rounded = (share * (1.0 / jnp.sum(share, axis=-1, keepdims=True))).astype(bf16)
                mixed = dot(rounded, v, ((1,), (0,)))
                attended[rows, lanes] = mixed.astype(bf16)
                store_turned(attended_t, real, rows, mixed.T.astype(bf16))
                share = rounded.astype(f32)
                grad = dot(up, v, ((1,), (1,)))
                centre = jnp.sum(share * grad, axis=-1, keepdims=True)
                grad = (share * (grad - centre) * score_scale).astype(bf16)
                grad_query[rows, lanes] = dot(grad, k, ((1,), (0,))).astype(bf16)
                key_grad = dot(grad, q, ((0,), (0,)))
                value_grad = dot(rounded, up, ((0,), (0,)))
                for part in range(3):
                    piece = slice(part * WINDOW, (part + 1) * WINDOW)
                    for sums, term in ((key_grads, key_grad[piece]), (value_grads, value_grad[piece])):
                        before = sums[block + part]
                        sums[block + part] = term if before is None else before + term
            for which, sums in enumerate((key_grads, value_grads)):
                for block in range(blocks + 2):
                    rows = slice(block * WINDOW, (block + 1) * WINDOW)
                    grad_pair[which, rows, lanes] = sums[block].astype(bf16)

    def spot(lane, block):
        return sum(((block >> bit) & 1) * (outer >> (step + 1)) for step, bit in enumerate(orders[lane]))

    def base(lane, stage):
        total = 0
        for step in range(stage):
            total = total + bit_at(orders[lane][step]) * (outer >> (step + 1))
        return total

    def landing(stage):
        return outer - (outer >> stage)

    def leaving(lane, stage):
        return base(lane, stage) + (1 - bit_at(orders[lane][stage])) * (outer >> (stage + 1))

    def remote(source, target, send, recv, device):
        return pltpu.make_async_remote_copy(
            src_ref=source,
            dst_ref=target,
            send_sem=send,
            recv_sem=recv,
            device_id=device,
            device_id_type=pl.DeviceIdType.MESH,
        )

    def core_copy(mail, got, chunk):
        return remote(mail, got, core_send.at[chunk], core_recv.at[chunk], other_core)

    def stage_copy(held, landed, chunk, lane, stage):
        half = outer >> (stage + 1)
        return remote(
            held.at[lane, pl.ds(leaving(lane, stage), half)],
            landed.at[lane, pl.ds(landing(stage), half)],
            stage_send.at[chunk, lane, stage],
            stage_recv.at[chunk, lane, stage],
            partner(orders[lane][stage]),
        )

    def gathered(bufs, lane, stage, where, *index):
        held, got, landed = bufs
        total = held[lane, where, *index].astype(f32) + got[lane, where, *index].astype(f32)
        for step in range(stage):
            place = landing(step) + where - base(lane, step + 1)
            total = total + landed[lane, place, *index].astype(f32)
        return total

    def reduce_stage(bufs, chunk, lane, stage, inner):
        held, got, landed = bufs
        half = outer >> (stage + 1)
        start = leaving(lane, stage)

        def add(step, carry):
            where, index = start + step // inner, step % inner
            held[lane, where, index] = gathered(bufs, lane, stage, where, index).astype(bf16)
            return carry

        lax.fori_loop(0, half * inner, add, 0)
        stage_copy(held, landed, chunk, lane, stage).start()

    def wait_stage(bufs, mail, chunk, lane, stage):
        held, got, landed = bufs
        if stage == 0:
            if lane == 0:
                core_copy(mail, got, chunk).wait()
        else:
            stage_copy(held, landed, chunk, lane, stage - 1).wait()

    def owner(pair, member):
        return (pair + member * pairs) // heads_each

    def tile_copy(pair, lane, member, away):
        return remote(
            held.at[pair, lane, base(lane, levels), member],
            last.at[pair, lane, member, away - 1],
            last_send.at[pair, lane, member],
            last_recv.at[pair, lane, member, away - 1],
            (seq, owner(pair, member)),
        )

    def advance(pair, stage):
        bufs = held.at[pair], got.at[pair], landed.at[pair]
        for lane in range(2):
            wait_stage(bufs, mail.at[pair], pair, lane, stage)
            if stage < levels:
                reduce_stage(bufs, pair, lane, stage, 2)
                continue
            where = base(lane, levels)
            for member in range(2):
                held[pair, lane, where, member] = gathered(bufs, lane, stage, where, member).astype(bf16)

                @pl.when(owner(pair, member) != head)
                def _():
                    tile_copy(pair, lane, member, (head - owner(pair, member) + head_size) % head_size).start()

    def finish(pair):
        for member in range(2):
            mine = owner(pair, member) == head
            inside = ((pair + member * pairs) % heads_each) * HEAD_SIZE

            @pl.when(mine)
            def _():
                for lane in range(2):
                    total = held[pair, lane, base(lane, levels), member].astype(f32)
                    for away in range(1, head_size):
                        tile_copy(pair, lane, member, away).wait_recv()
                        total = total + last[pair, lane, member, away - 1].astype(f32)
                    rows = slice(lane * part_rows, (lane + 1) * part_rows)
                    grad_qkv[:, rows, pl.ds(pl.multiple_of(inside, HEAD_SIZE), HEAD_SIZE)] = total

            @pl.when(jnp.logical_not(mine))
            def _():
                for lane in range(2):
                    tile_copy(pair, lane, member, 1).wait_send()

    def last_copy(lane, step):
        return remote(
            held_out.at[lane, base(lane, levels), (head + step) % head_size],
            last_out.at[lane, step - 1],
            last_send_out.at[lane, step - 1],
            last_recv_out.at[lane, step - 1],
            along(step),
        )

    def advance_out(stage):
        bufs = held_out, got_out, landed_out
        for lane in range(2):
            wait_stage(bufs, mail_out, pairs, lane, stage)
            if stage < levels:
                reduce_stage(bufs, pairs, lane, stage, head_size)
                continue
            where = base(lane, levels)
            for step in range(1, head_size):
                other = (head + step) % head_size
                held_out[lane, where, other] = gathered(bufs, lane, stage, where, other).astype(bf16)
                last_copy(lane, step).start()

    def finish_out():
        bufs = held_out, got_out, landed_out
        for lane in range(2):
            total = gathered(bufs, lane, levels, base(lane, levels), head)
            for step in range(1, head_size):
                last_copy(lane, step).wait()
                total = total + last_out[lane, step - 1].astype(f32)
            grad_out[lane * part_rows : (lane + 1) * part_rows, :] = total

    whole = slice(0, 2 * WINDOW + length)

    def products(pair, target, parity):
        cols = pl.ds(pl.multiple_of(pair * wide, wide), wide)
        for which in range(3):
            right = grad_query[:, cols] if which == 0 else grad_pair[which - 1, :, cols]
            product = dot(normed_t[parity, :, own if which == 0 else whole], right, ((1,), (0,))).astype(bf16)
            for block in range(outer):
                for lane in range(2):
                    start = block * tile_rows + lane * part_rows
                    for member in range(2):
                        target[pair, lane, spot(lane, block), member, which] = product[
                            start : start + part_rows, member * HEAD_SIZE : (member + 1) * HEAD_SIZE
                        ]

    def products_out(target, parity):
        def one(index, carry):
            cols = pl.ds(pl.multiple_of(index * tile_cols, tile_cols), tile_cols)
            product = dot(attended_t[parity], cotangent[:, cols], ((1,), (0,))).astype(bf16)
            for block in range(outer):
                for lane in range(2):
                    start = block * tile_rows + lane * part_rows
                    target[lane, spot(lane, block), index] = product[start : start + part_rows]
            return carry

        lax.fori_loop(0, head_size, one, 0)

    def pair_back(rows, cols):
        term = dot(grad_pair[0, rows, :], w_qkv[1, cols, :], ((1,), (1,)))
        return term + dot(grad_pair[1, rows, :], w_qkv[2, cols, :], ((1,), (1,)))

    def norm_back(step, carry):
        rows = pl.ds(pl.multiple_of(step * few, few), few)
        unit, inverse = standardise(frames[rows, :].astype(f32))
        grad = grad_normed[rows, :].astype(bf16).astype(f32) * gain[...]
        average = jnp.mean(grad, axis=-1, keepdims=True)
        along_unit = jnp.mean(grad * unit, axis=-1, keepdims=True)
        grad = inverse * (grad - average - unit * along_unit)
        grad_frames[rows, :] = (cotangent[rows, :].astype(f32) + grad).astype(bf16)
        return carry

    def pair_step(pair, carry):
        attend(pair)
        products(pair, mail, 1 - core)
        core_copy(mail.at[pair], got.at[pair], pair).start()
        products(pair, held, core)
        for stage in range(levels, -1, -1):

            @pl.when(pair >= stage)
            def _():
                advance(pair - stage, stage)

        return carry

    lax.fori_loop(0, pairs, pair_step, 0)

    def drain(step):
        for stage in range(levels, -1, -1):
            pair = pairs + step - stage
            if pair < pairs:
                advance(pair, stage)
            elif pair == pairs:
                advance_out(stage)

    products_out(mail_out, 1 - core)
    core_copy(mail_out, got_out, pairs).start()
    products_out(held_out, core)
    drain(0)
    for side in range(2):
        start = side * (length + WINDOW)
        for strip_start in range(0, channels, strip):
            cols = slice(strip_start, strip_start + strip)
            edge_out[side, :, cols] = pair_back(slice(start, start + WINDOW), cols).astype(bf16)
        edge_copy(side).start()
    drain(1)
    for start in range(0, channels, strip):
        cols = slice(start, start + strip)
        mixed = dot(attended[...], w_out[:, cols], ((1,), (0,)))
        output[:, cols] = (frames[:, cols].astype(f32) + mixed).astype(bf16)
    for start in range(0, channels, strip):
        cols = slice(start, start + strip)
        grad_normed[:, cols] = pair_back(own, cols) + dot(grad_query[...], w_qkv[0, cols, :], ((1,), (1,)))
    for step in range(2, levels + 1):
        drain(step)
    edge_copy(0).wait()
    edge_copy(1).wait()
    grad_normed[:WINDOW, :] += edge_in[1].astype(f32)
    grad_normed[length - WINDOW :, :] += edge_in[0].astype(f32)
    lax.fori_loop(0, length // few, norm_back, 0)

    def finish_pair(pair, carry):
        finish(pair)
        return carry

    lax.fori_loop(0, pairs, finish_pair, 0)
    finish_out()


def deliver_kernel(scale, output, grad_frames, grad_qkv, grad_out, *targets):
    targets[0][...] = output[...]
    targets[1][...] = grad_frames[...]
    targets[2][...] = grad_qkv[...] * scale
    targets[3][...] = grad_out[...] * scale


def shards(frames, cotangent, norm_gain, w_qkv, w_out):
    length, channels = frames.shape
    seq_size, head_size = lax.axis_size("seq"), lax.axis_size("head")
    devices = seq_size * head_size
    bordered = length + 2 * WINDOW
    tile_rows, tile_cols = channels // seq_size, channels // head_size
    outer, pairs = seq_size // 2, channels // (2 * HEAD_SIZE)
    levels = len(bits_of(outer))
    pair_part = (2, 3, tile_rows // 2, HEAD_SIZE)
    out_part = (tile_rows // 2, tile_cols)
    bf16, f32 = jnp.bfloat16, jnp.float32
    vmem, anywhere = pl.BlockSpec(memory_space=pltpu.VMEM), pl.BlockSpec(memory_space=pl.ANY)
    dma = pltpu.SemaphoreType.DMA
    shapes = [
        jax.ShapeDtypeStruct((length, channels), bf16),
        jax.ShapeDtypeStruct((length, channels), bf16),
        jax.ShapeDtypeStruct((3, tile_rows, tile_cols), f32),
        jax.ShapeDtypeStruct((tile_rows, tile_cols), f32),
    ]
    results = pl.pallas_call(
        functools.partial(block_kernel, (seq_size, head_size)),
        out_shape=shapes,
        in_specs=[vmem, vmem, vmem, anywhere, anywhere],
        out_specs=[vmem] * 4,
        scratch_shapes=[
            pltpu.VMEM((3, channels, channels), bf16),
            pltpu.VMEM((channels, channels), bf16),
            pltpu.VMEM((length, channels), bf16),
            pltpu.VMEM((2, channels // 2, bordered), bf16),
            pltpu.VMEM((length, channels), bf16),
            pltpu.VMEM((bordered, channels), bf16),
            pltpu.VMEM((bordered, channels), bf16),
            pltpu.VMEM((length, channels), bf16),
            pltpu.VMEM((length, channels), bf16),
            pltpu.VMEM((2, channels // 2, length), bf16),
            pltpu.VMEM((length, channels), bf16),
            pltpu.VMEM((2, bordered, channels), bf16),
            pltpu.VMEM((2, WINDOW, channels), bf16),
            pltpu.VMEM((2, WINDOW, channels), bf16),
            pltpu.VMEM((length, channels), f32),
            pltpu.VMEM((2, WINDOW, channels), bf16),
            pltpu.VMEM((2 * WINDOW, channels), bf16),
            pltpu.VMEM((pairs, 2, outer, *pair_part), bf16),
            pltpu.VMEM((pairs, 2, outer, *pair_part), bf16),
            pltpu.VMEM((pairs, 2, outer, *pair_part), bf16),
            pltpu.VMEM((pairs, 2, outer - 1, *pair_part), bf16),
            pltpu.VMEM((pairs, 2, 2, head_size - 1, *pair_part[1:]), bf16),
            pltpu.VMEM((2, outer, head_size, *out_part), bf16),
            pltpu.VMEM((2, outer, head_size, *out_part), bf16),
            pltpu.VMEM((2, outer, head_size, *out_part), bf16),
            pltpu.VMEM((2, outer - 1, head_size, *out_part), bf16),
            pltpu.VMEM((2, head_size - 1, *out_part), bf16),
            dma((4,)),
            dma((2,)),
            dma((2,)),
            dma((2,)),
            dma((2,)),
            dma((pairs + 1,)),
            dma((pairs + 1,)),
            dma((pairs + 1, 2, levels)),
            dma((pairs + 1, 2, levels)),
            dma((pairs, 2, 2)),
            dma((pairs, 2, 2, head_size - 1)),
            dma((2, head_size - 1)),
            dma((2, head_size - 1)),
        ],
        compiler_params=pltpu.CompilerParams(
            collective_id=0, has_side_effects=True, vmem_limit_bytes=60 * 2**20
        ),
        name="block",
    )(frames, cotangent, norm_gain.reshape(1, channels), w_qkv, w_out)
    return tuple(
        pl.pallas_call(
            functools.partial(deliver_kernel, (devices * length) ** (-0.5)),
            out_shape=shapes,
            in_specs=[vmem] * 4,
            out_specs=[vmem] * 4,
            name="deliver",
        )(*results)
    )


def solution(mesh):
    in_specs = (P(("seq", "head"), None), P(("seq", "head"), None), P(), P(), P())
    out_specs = (
        P(("seq", "head"), None),
        P(("seq", "head"), None),
        P(None, "seq", "head"),
        P("seq", "head"),
    )
    return jax.shard_map(shards, mesh=mesh, in_specs=in_specs, out_specs=out_specs, check_vma=False)
```

```python
import functools

import jax
import jax.numpy as jnp
from jax import lax
from jax.experimental import pallas as pl
from jax.experimental.pallas import tpu as pltpu
from jax.sharding import PartitionSpec as P

HEAD_SIZE = 128
WINDOW = 128

EPSILON = 1e-05
MASKED = -1e30
AXES = ("seq", "head")


def dot(a, b, contract):
    return lax.dot_general(a, b, (contract, ((), ())), preferred_element_type=jnp.float32)


def bits_of(size):
    return list(range(size.bit_length() - 1))


def block_kernel(
    sizes,
    frames_hbm, cotangent_hbm, gain, w_qkv_hbm, w_out_hbm,
    output, grad_frames, grad_qkv, grad_out,
    frames, cotangent, w_qkv, w_out, normed, normed_t, query, key, value, upstream, attended, attended_t,
    grad_query, grad_pair, grad_sum, edge_out, edge_in, grad_normed, halo, halo_normed,
    mail, got, held, landed, last, mail_out, got_out, held_out, landed_out, last_out,
    rows_sem, weight_sem, halo_send, halo_recv, edge_send, edge_recv,
    core_send, core_recv, stage_send, stage_recv, last_send, last_recv, last_send_out, last_recv_out,
):
    seq_size, head_size = sizes
    devices = seq_size * head_size
    length, channels = frames_hbm.shape
    outer, part_rows, tile_cols = held_out.shape[1], held_out.shape[3], held_out.shape[4]
    tile_rows = 2 * part_rows
    bits = bits_of(outer)
    orders = (bits, bits[::-1])
    levels = len(bits)
    seq, head = lax.axis_index("seq"), lax.axis_index("head")
    core, row_block = seq % 2, seq // 2
    position = seq * head_size + head
    bf16, f32 = jnp.bfloat16, jnp.float32
    strip = min(256, channels)

    def neighbour(step):
        there = (position + step + devices) % devices
        return (there // head_size, there % head_size)

    def bit_at(bit):
        return (row_block // 2**bit) % 2

    def partner(bit):
        return (2 * (row_block + (1 - 2 * bit_at(bit)) * 2**bit) + core, head)

    def along(step):
        return (seq, (head + step) % head_size)

    wide = 2 * HEAD_SIZE
    pairs = channels // wide
    heads_each = tile_cols // HEAD_SIZE

    loads = [
        pltpu.make_async_copy(frames_hbm, frames, rows_sem.at[0]),
        pltpu.make_async_copy(cotangent_hbm, cotangent, rows_sem.at[1]),
    ]
    loads[0].start()

    def weight_wait(which):
        if which == 3:
            pltpu.make_async_copy(w_out_hbm, w_out, weight_sem.at[3]).wait()
        else:
            pltpu.make_async_copy(w_qkv_hbm.at[which], w_qkv.at[which], weight_sem.at[which]).wait()

    other_core = (2 * row_block + 1 - core, head)
    greeted = [other_core] + [partner(bit) for bit in bits]
    greeted += [along(step) for step in range(1, head_size)] + [neighbour(1), neighbour(-1)]
    barrier = pltpu.get_barrier_semaphore()
    for device in greeted:
        pl.semaphore_signal(barrier, inc=1, device_id=device, device_id_type=pl.DeviceIdType.MESH)
    pl.semaphore_wait(barrier, len(greeted))

    def halo_copy(side):
        rows = pl.ds(length - WINDOW, WINDOW) if side == 0 else pl.ds(0, WINDOW)
        return pltpu.make_async_remote_copy(
            src_ref=frames_hbm.at[rows],
            dst_ref=halo.at[side],
            send_sem=halo_send.at[side],
            recv_sem=halo_recv.at[side],
            device_id=neighbour(1 if side == 0 else -1),
            device_id_type=pl.DeviceIdType.MESH,
        )

    at_start, at_end = head == 0, head == head_size - 1
    pl.when(jnp.logical_not(at_end))(lambda: halo_copy(0).start())
    pl.when(jnp.logical_not(at_start))(lambda: halo_copy(1).start())
    near_side = (head == 0).astype(jnp.int32)
    loads[1].start()

    for slot in range(2 * pairs):
        real = slot // 2 + (slot % 2) * pairs
        there, here = pl.ds(real * HEAD_SIZE, HEAD_SIZE), pl.ds(slot * HEAD_SIZE, HEAD_SIZE)
        pltpu.make_async_copy(w_out_hbm.at[there], w_out.at[here], weight_sem.at[3]).start()
    for which in range(3):
        for slot in range(2 * pairs):
            real = slot // 2 + (slot % 2) * pairs
            there, here = pl.ds(real * HEAD_SIZE, HEAD_SIZE), pl.ds(slot * HEAD_SIZE, HEAD_SIZE)
            pltpu.make_async_copy(
                w_qkv_hbm.at[which, :, there], w_qkv.at[which, :, here], weight_sem.at[which]
            ).start()


    def send_far():
        @pl.when(at_end)
        def _():
            halo_copy(1).wait_send()
            halo_copy(0).start()

        @pl.when(at_start)
        def _():
            halo_copy(0).wait_send()
            halo_copy(1).start()

    def halo_wait(side):
        pltpu.make_async_remote_copy(
            src_ref=frames_hbm.at[pl.ds(0, WINDOW)],
            dst_ref=halo.at[side],
            send_sem=halo_send.at[side],
            recv_sem=halo_recv.at[side],
            device_id=neighbour(1),
            device_id_type=pl.DeviceIdType.MESH,
        ).wait_recv()

    def halo_sent():
        pl.when(jnp.logical_not(at_end))(lambda: halo_copy(1).wait_send())
        pl.when(jnp.logical_not(at_start))(lambda: halo_copy(0).wait_send())

    def standardise(values):
        average = jnp.mean(values, axis=-1, keepdims=True)
        centered = values - average
        variance = jnp.mean(centered * centered, axis=-1, keepdims=True)
        inverse = lax.rsqrt(variance + EPSILON)
        return centered * inverse, inverse

    few = 64

    def norm_rows(source, target, target_row, rows):
        def one(step, carry):
            values = source[pl.ds(pl.multiple_of(step * few, few), few), :].astype(f32)
            rounded = (standardise(values)[0] * gain[...]).astype(bf16)
            target[pl.ds(pl.multiple_of(target_row + step * few, few), few), :] = rounded
            return carry

        lax.fori_loop(0, rows // few, one, 0)

    def multiply_into(target, rows, left, weight, side):
        for start in range(0, channels, strip):
            cols = slice(start, start + strip)
            other = weight[:, cols] if side == 0 else weight[cols, :]
            target[rows, cols] = dot(left, other, ((1,), (side,))).astype(target.dtype)

    loads[0].wait()
    norm_rows(frames, normed, 0, length)
    own = slice(WINDOW, WINDOW + length)

    piece = min(128, tile_rows)

    def store_turned(target, first, cols, turned):
        for start in range(0, 128, piece):
            block = (first + start) // tile_rows
            down = (block // 2) * tile_rows + (first + start) % tile_rows
            target[block % 2, pl.ds(pl.multiple_of(down, piece), piece), cols] = turned[start : start + piece]

    def turn(source, row, place, rows):
        for start in range(0, rows, 128):
            for col in range(0, channels, 128):
                down = pl.ds(pl.multiple_of(row + start, 128), 128)
                cols = pl.ds(pl.multiple_of(place + start, 128), 128)
                tile = source[down, col : col + 128]
                store_turned(normed_t, col, cols, tile.astype(f32).T.astype(bf16))

    turn(normed, 0, WINDOW, length)
    weight_wait(3)
    loads[1].wait()
    everything = slice(0, length)
    multiply_into(upstream, everything, cotangent[...], w_out, 1)
    send_far()
    for which, target, rows in ((0, query, everything), (1, key, own), (2, value, own)):
        weight_wait(which)
        multiply_into(target, rows, normed[...], w_qkv.at[which], 0)

    def halo_rows(side):
        halo_wait(side)
        first = pl.multiple_of(side * WINDOW, WINDOW)
        start = pl.multiple_of(side * (length + WINDOW), WINDOW)
        norm_rows(halo.at[side], halo_normed, first, WINDOW)
        turn(halo_normed, first, start, WINDOW)

    def halo_project(side, cols):
        first = pl.multiple_of(side * WINDOW, WINDOW)
        start = pl.multiple_of(side * (length + WINDOW), WINDOW)
        for which, target in ((1, key), (2, value)):
            made = dot(halo_normed[pl.ds(first, WINDOW), :], w_qkv[which, :, cols], ((1,), (0,)))
            target[pl.ds(start, WINDOW), cols] = made.astype(bf16)

    def edge_copy(side):
        return pltpu.make_async_remote_copy(
            src_ref=edge_out.at[side],
            dst_ref=edge_in.at[side],
            send_sem=edge_send.at[side],
            recv_sem=edge_recv.at[side],
            device_id=neighbour(-1 if side == 0 else 1),
            device_id_type=pl.DeviceIdType.MESH,
        )

    blocks = length // WINDOW
    span = 3 * WINDOW
    score_scale = HEAD_SIZE ** (-0.5)
    row = lax.broadcasted_iota(jnp.int32, (WINDOW, span), 0)
    col = lax.broadcasted_iota(jnp.int32, (WINDOW, span), 1)
    near = (col >= row) & (col <= row + 2 * WINDOW)

    def attend(pair, block):
        for member in range(2):
            lane = pl.multiple_of(pair * wide + member * HEAD_SIZE, HEAD_SIZE)
            lanes = pl.ds(lane, HEAD_SIZE)
            real = (pair + member * pairs) * HEAD_SIZE
            start = pl.multiple_of(block * WINDOW, WINDOW)
            rows, keys = pl.ds(start, WINDOW), pl.ds(start, span)
            q, k, v, up = query[rows, lanes], key[keys, lanes], value[keys, lanes], upstream[rows, lanes]
            frame = position * length + (block - 1) * WINDOW + col
            allowed = near & (frame >= 0) & (frame < devices * length)
            scores = jnp.where(allowed, dot(q, k, ((1,), (1,))) * score_scale, MASKED)
            share = jnp.exp(scores - jnp.max(scores, axis=-1, keepdims=True))
            rounded = (share * (1.0 / jnp.sum(share, axis=-1, keepdims=True))).astype(bf16)
            mixed = dot(rounded, v, ((1,), (0,)))
            attended[rows, lanes] = mixed.astype(bf16)
            store_turned(attended_t, real, rows, mixed.T.astype(bf16))
            share = rounded.astype(f32)
            grad = dot(up, v, ((1,), (1,)))
            centre = jnp.sum(share * grad, axis=-1, keepdims=True)
            grad = (share * (grad - centre) * score_scale).astype(bf16)
            grad_query[rows, lanes] = dot(grad, k, ((1,), (0,))).astype(bf16)
            grad_sum[0, keys, lanes] += dot(grad, q, ((0,), (0,)))
            grad_sum[1, keys, lanes] += dot(rounded, up, ((0,), (0,)))

    def near_step(pair, carry):
        cols = pl.ds(pl.multiple_of(pair * wide, wide), wide)
        grad_sum[:, :, cols] = jnp.zeros((2, length + 2 * WINDOW, wide), f32)
        halo_project(near_side, cols)
        for step in range(blocks - 1):
            attend(pair, near_side + step)
        return carry

    def spot(lane, block):
        return sum(((block >> bit) & 1) * (outer >> (step + 1)) for step, bit in enumerate(orders[lane]))

    def base(lane, stage):
        total = 0
        for step in range(stage):
            total = total + bit_at(orders[lane][step]) * (outer >> (step + 1))
        return total

    def landing(stage):
        return outer - (outer >> stage)

    def leaving(lane, stage):
        return base(lane, stage) + (1 - bit_at(orders[lane][stage])) * (outer >> (stage + 1))

    def remote(source, target, send, recv, device):
        return pltpu.make_async_remote_copy(
            src_ref=source,
            dst_ref=target,
            send_sem=send,
            recv_sem=recv,
            device_id=device,
            device_id_type=pl.DeviceIdType.MESH,
        )

    def core_copy(mail, got, chunk):
        return remote(mail, got, core_send.at[chunk], core_recv.at[chunk], other_core)

    def stage_copy(held, landed, chunk, lane, stage):
        half = outer >> (stage + 1)
        return remote(
            held.at[lane, pl.ds(leaving(lane, stage), half)],
            landed.at[lane, pl.ds(landing(stage), half)],
            stage_send.at[chunk, lane, stage],
            stage_recv.at[chunk, lane, stage],
            partner(orders[lane][stage]),
        )

    def gathered(bufs, lane, stage, where, *index):
        held, got, landed = bufs
        total = held[lane, where, *index].astype(f32) + got[lane, where, *index].astype(f32)
        for step in range(stage):
            place = landing(step) + where - base(lane, step + 1)
            total = total + landed[lane, place, *index].astype(f32)
        return total

    def reduce_stage(bufs, chunk, lane, stage, inner):
        held, got, landed = bufs
        half = outer >> (stage + 1)
        start = leaving(lane, stage)

        def add(step, carry):
            where, index = start + step // inner, step % inner
            held[lane, where, index] = gathered(bufs, lane, stage, where, index).astype(bf16)
            return carry

        lax.fori_loop(0, half * inner, add, 0)
        stage_copy(held, landed, chunk, lane, stage).start()

    def wait_stage(bufs, mail, chunk, lane, stage):
        held, got, landed = bufs
        if stage == 0:
            if lane == 0:
                core_copy(mail, got, chunk).wait()
        else:
            stage_copy(held, landed, chunk, lane, stage - 1).wait()

    def owner(pair, member):
        return (pair + member * pairs) // heads_each

    def tile_copy(pair, lane, member, away):
        return remote(
            held.at[pair, lane, base(lane, levels), member],
            last.at[pair, lane, member, away - 1],
            last_send.at[pair, lane, member],
            last_recv.at[pair, lane, member, away - 1],
            (seq, owner(pair, member)),
        )

    def advance(pair, stage):
        bufs = held.at[pair], got.at[pair], landed.at[pair]
        for lane in range(2):
            wait_stage(bufs, mail.at[pair], pair, lane, stage)
            if stage < levels:
                reduce_stage(bufs, pair, lane, stage, 2)
                continue
            where = base(lane, levels)
            for member in range(2):
                held[pair, lane, where, member] = gathered(bufs, lane, stage, where, member).astype(bf16)

                @pl.when(owner(pair, member) != head)
                def _():
                    tile_copy(pair, lane, member, (head - owner(pair, member) + head_size) % head_size).start()

    def finish(pair):
        for member in range(2):
            mine = owner(pair, member) == head
            inside = ((pair + member * pairs) % heads_each) * HEAD_SIZE

            @pl.when(mine)
            def _():
                for lane in range(2):
                    total = held[pair, lane, base(lane, levels), member].astype(f32)
                    for away in range(1, head_size):
                        tile_copy(pair, lane, member, away).wait_recv()
                        total = total + last[pair, lane, member, away - 1].astype(f32)
                    rows = slice(lane * part_rows, (lane + 1) * part_rows)
                    grad_qkv[:, rows, pl.ds(pl.multiple_of(inside, HEAD_SIZE), HEAD_SIZE)] = total

            @pl.when(jnp.logical_not(mine))
            def _():
                for lane in range(2):
                    tile_copy(pair, lane, member, 1).wait_send()

    def last_copy(lane, step):
        return remote(
            held_out.at[lane, base(lane, levels), (head + step) % head_size],
            last_out.at[lane, step - 1],
            last_send_out.at[lane, step - 1],
            last_recv_out.at[lane, step - 1],
            along(step),
        )

    def advance_out(stage):
        bufs = held_out, got_out, landed_out
        for lane in range(2):
            wait_stage(bufs, mail_out, pairs, lane, stage)
            if stage < levels:
                reduce_stage(bufs, pairs, lane, stage, head_size)
                continue
            where = base(lane, levels)
            for step in range(1, head_size):
                other = (head + step) % head_size
                held_out[lane, where, other] = gathered(bufs, lane, stage, where, other).astype(bf16)
                last_copy(lane, step).start()

    def finish_out():
        bufs = held_out, got_out, landed_out
        for lane in range(2):
            total = gathered(bufs, lane, levels, base(lane, levels), head)
            for step in range(1, head_size):
                last_copy(lane, step).wait()
                total = total + last_out[lane, step - 1].astype(f32)
            grad_out[lane * part_rows : (lane + 1) * part_rows, :] = total

    whole = slice(0, 2 * WINDOW + length)

    def products(pair, target, parity):
        cols = pl.ds(pl.multiple_of(pair * wide, wide), wide)
        for which in range(3):
            right = grad_query[:, cols] if which == 0 else grad_pair[which - 1, :, cols]
            product = dot(normed_t[parity, :, own if which == 0 else whole], right, ((1,), (0,))).astype(bf16)
            for block in range(outer):
                for lane in range(2):
                    start = block * tile_rows + lane * part_rows
                    for member in range(2):
                        target[pair, lane, spot(lane, block), member, which] = product[
                            start : start + part_rows, member * HEAD_SIZE : (member + 1) * HEAD_SIZE
                        ]

    def products_out(target, parity):
        def one(index, carry):
            cols = pl.ds(pl.multiple_of(index * tile_cols, tile_cols), tile_cols)
            product = dot(attended_t[parity], cotangent[:, cols], ((1,), (0,))).astype(bf16)
            for block in range(outer):
                for lane in range(2):
                    start = block * tile_rows + lane * part_rows
                    target[lane, spot(lane, block), index] = product[start : start + part_rows]
            return carry

        lax.fori_loop(0, head_size, one, 0)

    def pair_back(rows, cols):
        term = dot(grad_pair[0, rows, :], w_qkv[1, cols, :], ((1,), (1,)))
        return term + dot(grad_pair[1, rows, :], w_qkv[2, cols, :], ((1,), (1,)))

    def norm_back(step, carry):
        rows = pl.ds(pl.multiple_of(step * few, few), few)
        unit, inverse = standardise(frames[rows, :].astype(f32))
        grad = grad_normed[rows, :].astype(bf16).astype(f32) * gain[...]
        average = jnp.mean(grad, axis=-1, keepdims=True)
        along_unit = jnp.mean(grad * unit, axis=-1, keepdims=True)
        grad = inverse * (grad - average - unit * along_unit)
        grad_frames[rows, :] = (cotangent[rows, :].astype(f32) + grad).astype(bf16)
        return carry

    def pair_step(pair, carry):
        cols = pl.ds(pl.multiple_of(pair * wide, wide), wide)
        halo_project(1 - near_side, cols)
        attend(pair, (1 - near_side) * (blocks - 1))
        grad_pair[:, :, cols] = grad_sum[:, :, cols].astype(bf16)
        products(pair, mail, 1 - core)
        core_copy(mail.at[pair], got.at[pair], pair).start()
        products(pair, held, core)

        @pl.when(pair < pairs - 1)
        def _():
            near_step(pair + 1, 0)

        for stage in range(levels + 1):

            @pl.when(pair >= stage)
            def _():
                advance(pair - stage, stage)

        return carry

    halo_rows(near_side)
    lax.fori_loop(0, 1, near_step, 0)
    halo_rows(1 - near_side)
    halo_sent()
    lax.fori_loop(0, pairs, pair_step, 0)

    def drain(step):
        for stage in range(levels, -1, -1):
            pair = pairs + step - stage
            if pair < pairs:
                advance(pair, stage)
            elif pair == pairs:
                advance_out(stage)

    for side in range(2):
        start = side * (length + WINDOW)
        for strip_start in range(0, channels, strip):
            cols = slice(strip_start, strip_start + strip)
            edge_out[side, :, cols] = pair_back(slice(start, start + WINDOW), cols).astype(bf16)
        edge_copy(side).start()
    products_out(mail_out, 1 - core)
    core_copy(mail_out, got_out, pairs).start()
    products_out(held_out, core)
    drain(0)
    drain(1)
    for start in range(0, channels, strip):
        cols = slice(start, start + strip)
        mixed = dot(attended[...], w_out[:, cols], ((1,), (0,)))
        output[:, cols] = (frames[:, cols].astype(f32) + mixed).astype(bf16)
    for start in range(0, channels, strip):
        cols = slice(start, start + strip)
        grad_normed[:, cols] = pair_back(own, cols) + dot(grad_query[...], w_qkv[0, cols, :], ((1,), (1,)))
    for step in range(2, levels + 1):
        drain(step)
    edge_copy(0).wait()
    edge_copy(1).wait()
    grad_normed[:WINDOW, :] += edge_in[1].astype(f32)
    grad_normed[length - WINDOW :, :] += edge_in[0].astype(f32)
    lax.fori_loop(0, length // few, norm_back, 0)

    def finish_pair(pair, carry):
        finish(pair)
        return carry

    lax.fori_loop(0, pairs, finish_pair, 0)
    finish_out()


def deliver_kernel(scale, output, grad_frames, grad_qkv, grad_out, *targets):
    targets[0][...] = output[...]
    targets[1][...] = grad_frames[...]
    targets[2][...] = grad_qkv[...] * scale
    targets[3][...] = grad_out[...] * scale


def shards(frames, cotangent, norm_gain, w_qkv, w_out):
    length, channels = frames.shape
    seq_size, head_size = lax.axis_size("seq"), lax.axis_size("head")
    devices = seq_size * head_size
    bordered = length + 2 * WINDOW
    tile_rows, tile_cols = channels // seq_size, channels // head_size
    outer, pairs = seq_size // 2, channels // (2 * HEAD_SIZE)
    levels = len(bits_of(outer))
    pair_part = (2, 3, tile_rows // 2, HEAD_SIZE)
    out_part = (tile_rows // 2, tile_cols)
    bf16, f32 = jnp.bfloat16, jnp.float32
    vmem, anywhere = pl.BlockSpec(memory_space=pltpu.VMEM), pl.BlockSpec(memory_space=pl.ANY)
    dma = pltpu.SemaphoreType.DMA
    shapes = [
        jax.ShapeDtypeStruct((length, channels), bf16),
        jax.ShapeDtypeStruct((length, channels), bf16),
        jax.ShapeDtypeStruct((3, tile_rows, tile_cols), f32),
        jax.ShapeDtypeStruct((tile_rows, tile_cols), f32),
    ]
    results = pl.pallas_call(
        functools.partial(block_kernel, (seq_size, head_size)),
        out_shape=shapes,
        in_specs=[anywhere, anywhere, vmem, anywhere, anywhere],
        out_specs=[vmem] * 4,
        scratch_shapes=[
            pltpu.VMEM((length, channels), bf16),
            pltpu.VMEM((length, channels), bf16),
            pltpu.VMEM((3, channels, channels), bf16),
            pltpu.VMEM((channels, channels), bf16),
            pltpu.VMEM((length, channels), bf16),
            pltpu.VMEM((2, channels // 2, bordered), bf16),
            pltpu.VMEM((length, channels), bf16),
            pltpu.VMEM((bordered, channels), bf16),
            pltpu.VMEM((bordered, channels), bf16),
            pltpu.VMEM((length, channels), bf16),
            pltpu.VMEM((length, channels), bf16),
            pltpu.VMEM((2, channels // 2, length), bf16),
            pltpu.VMEM((length, channels), bf16),
            pltpu.VMEM((2, bordered, channels), bf16),
            pltpu.VMEM((2, bordered, channels), f32),
            pltpu.VMEM((2, WINDOW, channels), bf16),
            pltpu.VMEM((2, WINDOW, channels), bf16),
            pltpu.VMEM((length, channels), f32),
            pltpu.VMEM((2, WINDOW, channels), bf16),
            pltpu.VMEM((2 * WINDOW, channels), bf16),
            pltpu.VMEM((pairs, 2, outer, *pair_part), bf16),
            pltpu.VMEM((pairs, 2, outer, *pair_part), bf16),
            pltpu.VMEM((pairs, 2, outer, *pair_part), bf16),
            pltpu.VMEM((pairs, 2, outer - 1, *pair_part), bf16),
            pltpu.VMEM((pairs, 2, 2, head_size - 1, *pair_part[1:]), bf16),
            pltpu.VMEM((2, outer, head_size, *out_part), bf16),
            pltpu.VMEM((2, outer, head_size, *out_part), bf16),
            pltpu.VMEM((2, outer, head_size, *out_part), bf16),
            pltpu.VMEM((2, outer - 1, head_size, *out_part), bf16),
            pltpu.VMEM((2, head_size - 1, *out_part), bf16),
            dma((2,)),
            dma((4,)),
            dma((2,)),
            dma((2,)),
            dma((2,)),
            dma((2,)),
            dma((pairs + 1,)),
            dma((pairs + 1,)),
            dma((pairs + 1, 2, levels)),
            dma((pairs + 1, 2, levels)),
            dma((pairs, 2, 2)),
            dma((pairs, 2, 2, head_size - 1)),
            dma((2, head_size - 1)),
            dma((2, head_size - 1)),
        ],
        compiler_params=pltpu.CompilerParams(
            collective_id=0, has_side_effects=True, vmem_limit_bytes=60 * 2**20
        ),
        name="block",
    )(frames, cotangent, norm_gain.reshape(1, channels), w_qkv, w_out)
    return tuple(
        pl.pallas_call(
            functools.partial(deliver_kernel, (devices * length) ** (-0.5)),
            out_shape=shapes,
            in_specs=[vmem] * 4,
            out_specs=[vmem] * 4,
            name="deliver",
        )(*results)
    )


def solution(mesh):
    in_specs = (P(("seq", "head"), None), P(("seq", "head"), None), P(), P(), P())
    out_specs = (
        P(("seq", "head"), None),
        P(("seq", "head"), None),
        P(None, "seq", "head"),
        P("seq", "head"),
    )
    return jax.shard_map(shards, mesh=mesh, in_specs=in_specs, out_specs=out_specs, check_vma=False)
```

```python
import functools

import jax
import jax.numpy as jnp
from jax import lax
from jax.experimental import pallas as pl
from jax.experimental.pallas import tpu as pltpu
from jax.sharding import PartitionSpec as P

HEAD_SIZE = 128
WINDOW = 128

EPSILON = 1e-05
MASKED = -1e30
AXES = ("seq", "head")


def dot(a, b, contract):
    return lax.dot_general(a, b, (contract, ((), ())), preferred_element_type=jnp.float32)


def bits_of(size):
    return list(range(size.bit_length() - 1))


def block_kernel(
    sizes,
    frames_hbm, cotangent_hbm, gain, w_qkv_hbm, w_out_hbm,
    output, grad_frames, grad_qkv, grad_out,
    frames, cotangent, w_qkv, w_out, normed, normed_t, query, key, value, upstream, attended, attended_t,
    grad_query, grad_pair, grad_sum, edge_out, edge_in, grad_normed, halo, halo_normed,
    mail, got, held, landed, last, mail_out, got_out, held_out, landed_out, last_out,
    rows_sem, weight_sem, halo_send, halo_recv, edge_send, edge_recv,
    core_send, core_recv, stage_send, stage_recv, last_send, last_recv, last_send_out, last_recv_out,
):
    seq_size, head_size = sizes
    devices = seq_size * head_size
    length, channels = frames_hbm.shape
    outer, part_rows, tile_cols = held_out.shape[1], held_out.shape[3], held_out.shape[4]
    tile_rows = 2 * part_rows
    bits = bits_of(outer)
    orders = (bits, bits[::-1])
    levels = len(bits)
    seq, head = lax.axis_index("seq"), lax.axis_index("head")
    core, row_block = seq % 2, seq // 2
    position = seq * head_size + head
    bf16, f32 = jnp.bfloat16, jnp.float32
    strip = min(256, channels)

    def neighbour(step):
        there = (position + step + devices) % devices
        return (there // head_size, there % head_size)

    def bit_at(bit):
        return (row_block // 2**bit) % 2

    def partner(bit):
        return (2 * (row_block + (1 - 2 * bit_at(bit)) * 2**bit) + core, head)

    def along(step):
        return (seq, (head + step) % head_size)

    wide = 2 * HEAD_SIZE
    pairs = channels // wide
    heads_each = tile_cols // HEAD_SIZE

    loads = [
        pltpu.make_async_copy(frames_hbm, frames, rows_sem.at[0]),
        pltpu.make_async_copy(cotangent_hbm, cotangent, rows_sem.at[1]),
    ]
    loads[0].start()

    def weight_wait(which):
        if which == 3:
            pltpu.make_async_copy(w_out_hbm, w_out, weight_sem.at[3]).wait()
        else:
            pltpu.make_async_copy(w_qkv_hbm.at[which], w_qkv.at[which], weight_sem.at[which]).wait()

    other_core = (2 * row_block + 1 - core, head)
    greeted = [other_core] + [partner(bit) for bit in bits]
    greeted += [along(step) for step in range(1, head_size)] + [neighbour(1), neighbour(-1)]
    barrier = pltpu.get_barrier_semaphore()
    for device in greeted:
        pl.semaphore_signal(barrier, inc=1, device_id=device, device_id_type=pl.DeviceIdType.MESH)
    pl.semaphore_wait(barrier, len(greeted))

    def halo_copy(side):
        rows = pl.ds(length - WINDOW, WINDOW) if side == 0 else pl.ds(0, WINDOW)
        return pltpu.make_async_remote_copy(
            src_ref=frames_hbm.at[rows],
            dst_ref=halo.at[side],
            send_sem=halo_send.at[side],
            recv_sem=halo_recv.at[side],
            device_id=neighbour(1 if side == 0 else -1),
            device_id_type=pl.DeviceIdType.MESH,
        )

    at_start, at_end = head == 0, head == head_size - 1
    pl.when(jnp.logical_not(at_end))(lambda: halo_copy(0).start())
    pl.when(jnp.logical_not(at_start))(lambda: halo_copy(1).start())
    near_side = (head == 0).astype(jnp.int32)
    loads[1].start()

    for slot in range(2 * pairs):
        real = slot // 2 + (slot % 2) * pairs
        there, here = pl.ds(real * HEAD_SIZE, HEAD_SIZE), pl.ds(slot * HEAD_SIZE, HEAD_SIZE)
        pltpu.make_async_copy(w_out_hbm.at[there], w_out.at[here], weight_sem.at[3]).start()
    for which in range(3):
        for slot in range(2 * pairs):
            real = slot // 2 + (slot % 2) * pairs
            there, here = pl.ds(real * HEAD_SIZE, HEAD_SIZE), pl.ds(slot * HEAD_SIZE, HEAD_SIZE)
            pltpu.make_async_copy(
                w_qkv_hbm.at[which, :, there], w_qkv.at[which, :, here], weight_sem.at[which]
            ).start()


    def send_far():
        @pl.when(at_end)
        def _():
            halo_copy(1).wait_send()
            halo_copy(0).start()

        @pl.when(at_start)
        def _():
            halo_copy(0).wait_send()
            halo_copy(1).start()

    def halo_wait(side):
        pltpu.make_async_remote_copy(
            src_ref=frames_hbm.at[pl.ds(0, WINDOW)],
            dst_ref=halo.at[side],
            send_sem=halo_send.at[side],
            recv_sem=halo_recv.at[side],
            device_id=neighbour(1),
            device_id_type=pl.DeviceIdType.MESH,
        ).wait_recv()

    def halo_sent():
        pl.when(jnp.logical_not(at_end))(lambda: halo_copy(1).wait_send())
        pl.when(jnp.logical_not(at_start))(lambda: halo_copy(0).wait_send())

    def standardise(values):
        average = jnp.mean(values, axis=-1, keepdims=True)
        centered = values - average
        variance = jnp.mean(centered * centered, axis=-1, keepdims=True)
        inverse = lax.rsqrt(variance + EPSILON)
        return centered * inverse, inverse

    few = 64

    def norm_rows(source, target, target_row, rows):
        def one(step, carry):
            values = source[pl.ds(pl.multiple_of(step * few, few), few), :].astype(f32)
            rounded = (standardise(values)[0] * gain[...]).astype(bf16)
            target[pl.ds(pl.multiple_of(target_row + step * few, few), few), :] = rounded
            return carry

        lax.fori_loop(0, rows // few, one, 0)

    def multiply_into(target, rows, left, weight, side):
        for start in range(0, channels, strip):
            cols = slice(start, start + strip)
            other = weight[:, cols] if side == 0 else weight[cols, :]
            target[rows, cols] = dot(left, other, ((1,), (side,))).astype(target.dtype)

    loads[0].wait()
    norm_rows(frames, normed, 0, length)
    own = slice(WINDOW, WINDOW + length)

    piece = min(128, tile_rows)

    def store_turned(target, first, cols, turned):
        for start in range(0, 128, piece):
            block = (first + start) // tile_rows
            down = (block // 2) * tile_rows + (first + start) % tile_rows
            target[block % 2, pl.ds(pl.multiple_of(down, piece), piece), cols] = turned[start : start + piece]

    def turn(source, row, place, rows):
        for start in range(0, rows, 128):
            for col in range(0, channels, 128):
                down = pl.ds(pl.multiple_of(row + start, 128), 128)
                cols = pl.ds(pl.multiple_of(place + start, 128), 128)
                tile = source[down, col : col + 128]
                store_turned(normed_t, col, cols, tile.astype(f32).T.astype(bf16))

    turn(normed, 0, WINDOW, length)
    weight_wait(3)
    loads[1].wait()
    everything = slice(0, length)
    multiply_into(upstream, everything, cotangent[...], w_out, 1)
    send_far()
    for which, target, rows in ((0, query, everything), (1, key, own), (2, value, own)):
        weight_wait(which)
        multiply_into(target, rows, normed[...], w_qkv.at[which], 0)

    def halo_rows(side):
        halo_wait(side)
        first = pl.multiple_of(side * WINDOW, WINDOW)
        start = pl.multiple_of(side * (length + WINDOW), WINDOW)
        norm_rows(halo.at[side], halo_normed, first, WINDOW)
        turn(halo_normed, first, start, WINDOW)

    def halo_project(side, cols):
        first = pl.multiple_of(side * WINDOW, WINDOW)
        start = pl.multiple_of(side * (length + WINDOW), WINDOW)
        for which, target in ((1, key), (2, value)):
            made = dot(halo_normed[pl.ds(first, WINDOW), :], w_qkv[which, :, cols], ((1,), (0,)))
            target[pl.ds(start, WINDOW), cols] = made.astype(bf16)

    def edge_copy(side):
        return pltpu.make_async_remote_copy(
            src_ref=edge_out.at[side],
            dst_ref=edge_in.at[side],
            send_sem=edge_send.at[side],
            recv_sem=edge_recv.at[side],
            device_id=neighbour(-1 if side == 0 else 1),
            device_id_type=pl.DeviceIdType.MESH,
        )

    blocks = length // WINDOW
    span = 3 * WINDOW
    score_scale = HEAD_SIZE ** (-0.5)
    row = lax.broadcasted_iota(jnp.int32, (WINDOW, span), 0)
    col = lax.broadcasted_iota(jnp.int32, (WINDOW, span), 1)
    near = (col >= row) & (col <= row + 2 * WINDOW)

    def attend(pair, block):
        for member in range(2):
            lane = pl.multiple_of(pair * wide + member * HEAD_SIZE, HEAD_SIZE)
            lanes = pl.ds(lane, HEAD_SIZE)
            real = (pair + member * pairs) * HEAD_SIZE
            start = pl.multiple_of(block * WINDOW, WINDOW)
            rows, keys = pl.ds(start, WINDOW), pl.ds(start, span)
            q, k, v, up = query[rows, lanes], key[keys, lanes], value[keys, lanes], upstream[rows, lanes]
            frame = position * length + (block - 1) * WINDOW + col
            allowed = near & (frame >= 0) & (frame < devices * length)
            scores = jnp.where(allowed, dot(q, k, ((1,), (1,))) * score_scale, MASKED)
            share = jnp.exp(scores - jnp.max(scores, axis=-1, keepdims=True))
            rounded = (share * (1.0 / jnp.sum(share, axis=-1, keepdims=True))).astype(bf16)
            mixed = dot(rounded, v, ((1,), (0,)))
            attended[rows, lanes] = mixed.astype(bf16)
            store_turned(attended_t, real, rows, mixed.T.astype(bf16))
            share = rounded.astype(f32)
            grad = dot(up, v, ((1,), (1,)))
            centre = jnp.sum(share * grad, axis=-1, keepdims=True)
            grad = (share * (grad - centre) * score_scale).astype(bf16)
            grad_query[rows, lanes] = dot(grad, k, ((1,), (0,))).astype(bf16)
            grad_sum[0, keys, lanes] += dot(grad, q, ((0,), (0,)))
            grad_sum[1, keys, lanes] += dot(rounded, up, ((0,), (0,)))

    def near_step(pair, carry):
        cols = pl.ds(pl.multiple_of(pair * wide, wide), wide)
        grad_sum[:, :, cols] = jnp.zeros((2, length + 2 * WINDOW, wide), f32)
        halo_project(near_side, cols)
        for step in range(blocks - 1):
            attend(pair, near_side + step)
        return carry

    def spot(lane, block):
        return sum(((block >> bit) & 1) * (outer >> (step + 1)) for step, bit in enumerate(orders[lane]))

    def base(lane, stage):
        total = 0
        for step in range(stage):
            total = total + bit_at(orders[lane][step]) * (outer >> (step + 1))
        return total

    def landing(stage):
        return outer - (outer >> stage)

    def leaving(lane, stage):
        return base(lane, stage) + (1 - bit_at(orders[lane][stage])) * (outer >> (stage + 1))

    def remote(source, target, send, recv, device):
        return pltpu.make_async_remote_copy(
            src_ref=source,
            dst_ref=target,
            send_sem=send,
            recv_sem=recv,
            device_id=device,
            device_id_type=pl.DeviceIdType.MESH,
        )

    def core_copy(mail, got, chunk):
        return remote(mail, got, core_send.at[chunk], core_recv.at[chunk], other_core)

    def stage_copy(held, landed, chunk, lane, stage):
        half = outer >> (stage + 1)
        return remote(
            held.at[lane, pl.ds(leaving(lane, stage), half)],
            landed.at[lane, pl.ds(landing(stage), half)],
            stage_send.at[chunk, lane, stage],
            stage_recv.at[chunk, lane, stage],
            partner(orders[lane][stage]),
        )

    def gathered(bufs, lane, stage, where, *index):
        held, got, landed = bufs
        total = held[lane, where, *index].astype(f32) + got[lane, where, *index].astype(f32)
        for step in range(stage):
            place = landing(step) + where - base(lane, step + 1)
            total = total + landed[lane, place, *index].astype(f32)
        return total

    def reduce_stage(bufs, chunk, lane, stage, inner):
        held, got, landed = bufs
        half = outer >> (stage + 1)
        start = leaving(lane, stage)

        def add(step, carry):
            where, index = start + step // inner, step % inner
            held[lane, where, index] = gathered(bufs, lane, stage, where, index).astype(bf16)
            return carry

        lax.fori_loop(0, half * inner, add, 0)
        stage_copy(held, landed, chunk, lane, stage).start()

    def wait_stage(bufs, mail, chunk, lane, stage):
        held, got, landed = bufs
        if stage == 0:
            if lane == 0:
                core_copy(mail, got, chunk).wait()
        else:
            stage_copy(held, landed, chunk, lane, stage - 1).wait()

    def owner(pair, member):
        return (pair + member * pairs) // heads_each

    def tile_copy(pair, lane, member, away):
        return remote(
            held.at[pair, lane, base(lane, levels), member],
            last.at[pair, lane, member, away - 1],
            last_send.at[pair, lane, member],
            last_recv.at[pair, lane, member, away - 1],
            (seq, owner(pair, member)),
        )

    def advance(pair, stage):
        bufs = held.at[pair], got.at[pair], landed.at[pair]
        for lane in range(2):
            wait_stage(bufs, mail.at[pair], pair, lane, stage)
            if stage < levels:
                reduce_stage(bufs, pair, lane, stage, 2)
                continue
            where = base(lane, levels)
            for member in range(2):
                held[pair, lane, where, member] = gathered(bufs, lane, stage, where, member).astype(bf16)

                @pl.when(owner(pair, member) != head)
                def _():
                    tile_copy(pair, lane, member, (head - owner(pair, member) + head_size) % head_size).start()

    def finish(pair):
        for member in range(2):
            mine = owner(pair, member) == head
            inside = ((pair + member * pairs) % heads_each) * HEAD_SIZE

            @pl.when(mine)
            def _():
                for lane in range(2):
                    total = held[pair, lane, base(lane, levels), member].astype(f32)
                    for away in range(1, head_size):
                        tile_copy(pair, lane, member, away).wait_recv()
                        total = total + last[pair, lane, member, away - 1].astype(f32)
                    rows = slice(lane * part_rows, (lane + 1) * part_rows)
                    grad_qkv[:, rows, pl.ds(pl.multiple_of(inside, HEAD_SIZE), HEAD_SIZE)] = total

            @pl.when(jnp.logical_not(mine))
            def _():
                for lane in range(2):
                    tile_copy(pair, lane, member, 1).wait_send()

    def last_copy(lane, step):
        return remote(
            held_out.at[lane, base(lane, levels), (head + step) % head_size],
            last_out.at[lane, step - 1],
            last_send_out.at[lane, step - 1],
            last_recv_out.at[lane, step - 1],
            along(step),
        )

    def advance_out(stage):
        bufs = held_out, got_out, landed_out
        for lane in range(2):
            wait_stage(bufs, mail_out, pairs, lane, stage)
            if stage < levels:
                reduce_stage(bufs, pairs, lane, stage, head_size)
                continue
            where = base(lane, levels)
            for step in range(1, head_size):
                other = (head + step) % head_size
                held_out[lane, where, other] = gathered(bufs, lane, stage, where, other).astype(bf16)
                last_copy(lane, step).start()

    def finish_out():
        bufs = held_out, got_out, landed_out
        for lane in range(2):
            total = gathered(bufs, lane, levels, base(lane, levels), head)
            for step in range(1, head_size):
                last_copy(lane, step).wait()
                total = total + last_out[lane, step - 1].astype(f32)
            grad_out[lane * part_rows : (lane + 1) * part_rows, :] = total

    whole = slice(0, 2 * WINDOW + length)

    def products(pair, target, parity):
        cols = pl.ds(pl.multiple_of(pair * wide, wide), wide)
        for which in range(3):
            right = grad_query[:, cols] if which == 0 else grad_pair[which - 1, :, cols]
            product = dot(normed_t[parity, :, own if which == 0 else whole], right, ((1,), (0,))).astype(bf16)
            for block in range(outer):
                for lane in range(2):
                    start = block * tile_rows + lane * part_rows
                    for member in range(2):
                        target[pair, lane, spot(lane, block), member, which] = product[
                            start : start + part_rows, member * HEAD_SIZE : (member + 1) * HEAD_SIZE
                        ]

    def products_out(target, parity):
        def one(index, carry):
            cols = pl.ds(pl.multiple_of(index * tile_cols, tile_cols), tile_cols)
            product = dot(attended_t[parity], cotangent[:, cols], ((1,), (0,))).astype(bf16)
            for block in range(outer):
                for lane in range(2):
                    start = block * tile_rows + lane * part_rows
                    target[lane, spot(lane, block), index] = product[start : start + part_rows]
            return carry

        lax.fori_loop(0, head_size, one, 0)

    def pair_back(rows, cols):
        term = dot(grad_pair[0, rows, :], w_qkv[1, cols, :], ((1,), (1,)))
        return term + dot(grad_pair[1, rows, :], w_qkv[2, cols, :], ((1,), (1,)))

    def norm_back(step, carry):
        rows = pl.ds(pl.multiple_of(step * few, few), few)
        unit, inverse = standardise(frames[rows, :].astype(f32))
        grad = grad_normed[rows, :].astype(bf16).astype(f32) * gain[...]
        average = jnp.mean(grad, axis=-1, keepdims=True)
        along_unit = jnp.mean(grad * unit, axis=-1, keepdims=True)
        grad = inverse * (grad - average - unit * along_unit)
        grad_frames[rows, :] = (cotangent[rows, :].astype(f32) + grad).astype(bf16)
        return carry

    def send_edges():
        for side in range(2):
            start = side * (length + WINDOW)
            for strip_start in range(0, channels, strip):
                cols = slice(strip_start, strip_start + strip)
                edge_out[side, :, cols] = pair_back(slice(start, start + WINDOW), cols).astype(bf16)
            edge_copy(side).start()

    def far_step(pair):
        cols = pl.ds(pl.multiple_of(pair * wide, wide), wide)
        halo_project(1 - near_side, cols)
        attend(pair, (1 - near_side) * (blocks - 1))
        grad_pair[:, :, cols] = grad_sum[:, :, cols].astype(bf16)

    def pair_step(pair, carry):
        products(pair, mail, 1 - core)
        core_copy(mail.at[pair], got.at[pair], pair).start()
        products(pair, held, core)

        @pl.when(pair < pairs - 1)
        def _():
            far_step(pair + 1)

        @pl.when(pair == pairs - 1)
        def _():
            send_edges()

        for stage in range(levels + 1):

            @pl.when(pair >= stage)
            def _():
                advance(pair - stage, stage)

        @pl.when(pair == 1)
        def _():
            near_step(pairs - 1, 0)

        return carry

    halo_rows(near_side)
    lax.fori_loop(0, pairs - 1, near_step, 0)
    halo_rows(1 - near_side)
    halo_sent()
    far_step(0)
    lax.fori_loop(0, pairs, pair_step, 0)

    def drain(step):
        for stage in range(levels, -1, -1):
            pair = pairs + step - stage
            if pair < pairs:
                advance(pair, stage)
            elif pair == pairs:
                advance_out(stage)

    products_out(mail_out, 1 - core)
    core_copy(mail_out, got_out, pairs).start()
    products_out(held_out, core)
    drain(0)
    drain(1)
    for start in range(0, channels, strip):
        cols = slice(start, start + strip)
        mixed = dot(attended[...], w_out[:, cols], ((1,), (0,)))
        output[:, cols] = (frames[:, cols].astype(f32) + mixed).astype(bf16)
    for start in range(0, channels, strip):
        cols = slice(start, start + strip)
        grad_normed[:, cols] = pair_back(own, cols) + dot(grad_query[...], w_qkv[0, cols, :], ((1,), (1,)))
    for step in range(2, levels + 1):
        drain(step)
    edge_copy(0).wait()
    edge_copy(1).wait()
    grad_normed[:WINDOW, :] += edge_in[1].astype(f32)
    grad_normed[length - WINDOW :, :] += edge_in[0].astype(f32)
    lax.fori_loop(0, length // few, norm_back, 0)

    def finish_pair(pair, carry):
        finish(pair)
        return carry

    lax.fori_loop(0, pairs, finish_pair, 0)
    finish_out()


def deliver_kernel(scale, output, grad_frames, grad_qkv, grad_out, *targets):
    targets[0][...] = output[...]
    targets[1][...] = grad_frames[...]
    targets[2][...] = grad_qkv[...] * scale
    targets[3][...] = grad_out[...] * scale


def shards(frames, cotangent, norm_gain, w_qkv, w_out):
    length, channels = frames.shape
    seq_size, head_size = lax.axis_size("seq"), lax.axis_size("head")
    devices = seq_size * head_size
    bordered = length + 2 * WINDOW
    tile_rows, tile_cols = channels // seq_size, channels // head_size
    outer, pairs = seq_size // 2, channels // (2 * HEAD_SIZE)
    levels = len(bits_of(outer))
    pair_part = (2, 3, tile_rows // 2, HEAD_SIZE)
    out_part = (tile_rows // 2, tile_cols)
    bf16, f32 = jnp.bfloat16, jnp.float32
    vmem, anywhere = pl.BlockSpec(memory_space=pltpu.VMEM), pl.BlockSpec(memory_space=pl.ANY)
    dma = pltpu.SemaphoreType.DMA
    shapes = [
        jax.ShapeDtypeStruct((length, channels), bf16),
        jax.ShapeDtypeStruct((length, channels), bf16),
        jax.ShapeDtypeStruct((3, tile_rows, tile_cols), f32),
        jax.ShapeDtypeStruct((tile_rows, tile_cols), f32),
    ]
    results = pl.pallas_call(
        functools.partial(block_kernel, (seq_size, head_size)),
        out_shape=[pltpu.VMEM(one.shape, one.dtype) for one in shapes],
        in_specs=[anywhere, anywhere, vmem, anywhere, anywhere],
        out_specs=[vmem] * 4,
        scratch_shapes=[
            pltpu.VMEM((length, channels), bf16),
            pltpu.VMEM((length, channels), bf16),
            pltpu.VMEM((3, channels, channels), bf16),
            pltpu.VMEM((channels, channels), bf16),
            pltpu.VMEM((length, channels), bf16),
            pltpu.VMEM((2, channels // 2, bordered), bf16),
            pltpu.VMEM((length, channels), bf16),
            pltpu.VMEM((bordered, channels), bf16),
            pltpu.VMEM((bordered, channels), bf16),
            pltpu.VMEM((length, channels), bf16),
            pltpu.VMEM((length, channels), bf16),
            pltpu.VMEM((2, channels // 2, length), bf16),
            pltpu.VMEM((length, channels), bf16),
            pltpu.VMEM((2, bordered, channels), bf16),
            pltpu.VMEM((2, bordered, channels), f32),
            pltpu.VMEM((2, WINDOW, channels), bf16),
            pltpu.VMEM((2, WINDOW, channels), bf16),
            pltpu.VMEM((length, channels), f32),
            pltpu.VMEM((2, WINDOW, channels), bf16),
            pltpu.VMEM((2 * WINDOW, channels), bf16),
            pltpu.VMEM((pairs, 2, outer, *pair_part), bf16),
            pltpu.VMEM((pairs, 2, outer, *pair_part), bf16),
            pltpu.VMEM((pairs, 2, outer, *pair_part), bf16),
            pltpu.VMEM((pairs, 2, outer - 1, *pair_part), bf16),
            pltpu.VMEM((pairs, 2, 2, head_size - 1, *pair_part[1:]), bf16),
            pltpu.VMEM((2, outer, head_size, *out_part), bf16),
            pltpu.VMEM((2, outer, head_size, *out_part), bf16),
            pltpu.VMEM((2, outer, head_size, *out_part), bf16),
            pltpu.VMEM((2, outer - 1, head_size, *out_part), bf16),
            pltpu.VMEM((2, head_size - 1, *out_part), bf16),
            dma((2,)),
            dma((4,)),
            dma((2,)),
            dma((2,)),
            dma((2,)),
            dma((2,)),
            dma((pairs + 1,)),
            dma((pairs + 1,)),
            dma((pairs + 1, 2, levels)),
            dma((pairs + 1, 2, levels)),
            dma((pairs, 2, 2)),
            dma((pairs, 2, 2, head_size - 1)),
            dma((2, head_size - 1)),
            dma((2, head_size - 1)),
        ],
        compiler_params=pltpu.CompilerParams(
            collective_id=0, has_side_effects=True, vmem_limit_bytes=60 * 2**20
        ),
        name="block",
    )(frames, cotangent, norm_gain.reshape(1, channels), w_qkv, w_out)
    return tuple(
        pl.pallas_call(
            functools.partial(deliver_kernel, (devices * length) ** (-0.5)),
            out_shape=shapes,
            in_specs=[vmem] * 4,
            out_specs=[vmem] * 4,
            name="deliver",
        )(*[pltpu.with_memory_space_constraint(one, pltpu.VMEM) for one in results])
    )


def solution(mesh):
    in_specs = (P(("seq", "head"), None), P(("seq", "head"), None), P(), P(), P())
    out_specs = (
        P(("seq", "head"), None),
        P(("seq", "head"), None),
        P(None, "seq", "head"),
        P("seq", "head"),
    )
    return jax.shard_map(shards, mesh=mesh, in_specs=in_specs, out_specs=out_specs, check_vma=False)
```

```python
import functools

import jax
import jax.numpy as jnp
from jax import lax
from jax.experimental import pallas as pl
from jax.experimental.pallas import tpu as pltpu
from jax.sharding import PartitionSpec as P

HEAD_SIZE = 128
WINDOW = 128

EPSILON = 1e-05
MASKED = -1e30
AXES = ("seq", "head")


def dot(a, b, contract):
    return lax.dot_general(a, b, (contract, ((), ())), preferred_element_type=jnp.float32)


def bits_of(size):
    return list(range(size.bit_length() - 1))


def block_kernel(
    sizes,
    frames_hbm, cotangent_hbm, gain, w_qkv_hbm, w_out_hbm,
    output, grad_frames, grad_qkv, grad_out,
    frames, cotangent, w_qkv, w_out, normed, normed_t, query, key, value, upstream, attended, attended_t,
    grad_query, grad_pair, grad_sum, edge_out, edge_in, grad_normed, halo, halo_normed,
    mail, got, held, landed, last, mail_out, got_out, held_out, landed_out, last_out,
    rows_sem, weight_sem, halo_send, halo_recv, edge_send, edge_recv,
    core_send, core_recv, stage_send, stage_recv, last_send, last_recv, last_send_out, last_recv_out,
):
    seq_size, head_size = sizes
    devices = seq_size * head_size
    length, channels = frames_hbm.shape
    outer, part_rows, tile_cols = held_out.shape[1], held_out.shape[3], held_out.shape[4]
    tile_rows = 2 * part_rows
    bits = bits_of(outer)
    orders = (bits, bits[::-1])
    levels = len(bits)
    seq, head = lax.axis_index("seq"), lax.axis_index("head")
    core, row_block = seq % 2, seq // 2
    position = seq * head_size + head
    bf16, f32 = jnp.bfloat16, jnp.float32
    strip = min(256, channels)

    def neighbour(step):
        there = (position + step + devices) % devices
        return (there // head_size, there % head_size)

    def bit_at(bit):
        return (row_block // 2**bit) % 2

    def partner(bit):
        return (2 * (row_block + (1 - 2 * bit_at(bit)) * 2**bit) + core, head)

    def along(step):
        return (seq, (head + step) % head_size)

    wide = 2 * HEAD_SIZE
    pairs = channels // wide
    heads_each = tile_cols // HEAD_SIZE

    loads = [
        pltpu.make_async_copy(frames_hbm, frames, rows_sem.at[0]),
        pltpu.make_async_copy(cotangent_hbm, cotangent, rows_sem.at[1]),
    ]
    loads[0].start()

    def weight_wait(which):
        if which == 3:
            pltpu.make_async_copy(w_out_hbm, w_out, weight_sem.at[3]).wait()
        else:
            pltpu.make_async_copy(w_qkv_hbm.at[which], w_qkv.at[which], weight_sem.at[which]).wait()

    other_core = (2 * row_block + 1 - core, head)
    greeted = [other_core] + [partner(bit) for bit in bits]
    greeted += [along(step) for step in range(1, head_size)] + [neighbour(1), neighbour(-1)]
    barrier = pltpu.get_barrier_semaphore()
    for device in greeted:
        pl.semaphore_signal(barrier, inc=1, device_id=device, device_id_type=pl.DeviceIdType.MESH)
    pl.semaphore_wait(barrier, len(greeted))

    def halo_copy(side):
        rows = pl.ds(length - WINDOW, WINDOW) if side == 0 else pl.ds(0, WINDOW)
        return pltpu.make_async_remote_copy(
            src_ref=frames_hbm.at[rows],
            dst_ref=halo.at[side],
            send_sem=halo_send.at[side],
            recv_sem=halo_recv.at[side],
            device_id=neighbour(1 if side == 0 else -1),
            device_id_type=pl.DeviceIdType.MESH,
        )

    at_start, at_end = head == 0, head == head_size - 1
    pl.when(jnp.logical_not(at_end))(lambda: halo_copy(0).start())
    pl.when(jnp.logical_not(at_start))(lambda: halo_copy(1).start())
    near_side = (head == 0).astype(jnp.int32)
    loads[1].start()

    for slot in range(2 * pairs):
        real = (2 * pairs - 1 - slot // 2) if slot % 2 else slot // 2
        there, here = pl.ds(real * HEAD_SIZE, HEAD_SIZE), pl.ds(slot * HEAD_SIZE, HEAD_SIZE)
        pltpu.make_async_copy(w_out_hbm.at[there], w_out.at[here], weight_sem.at[3]).start()
    for which in range(3):
        for slot in range(2 * pairs):
            real = (2 * pairs - 1 - slot // 2) if slot % 2 else slot // 2
            there, here = pl.ds(real * HEAD_SIZE, HEAD_SIZE), pl.ds(slot * HEAD_SIZE, HEAD_SIZE)
            pltpu.make_async_copy(
                w_qkv_hbm.at[which, :, there], w_qkv.at[which, :, here], weight_sem.at[which]
            ).start()


    def send_far():
        @pl.when(at_end)
        def _():
            halo_copy(1).wait_send()
            halo_copy(0).start()

        @pl.when(at_start)
        def _():
            halo_copy(0).wait_send()
            halo_copy(1).start()

    def halo_wait(side):
        pltpu.make_async_remote_copy(
            src_ref=frames_hbm.at[pl.ds(0, WINDOW)],
            dst_ref=halo.at[side],
            send_sem=halo_send.at[side],
            recv_sem=halo_recv.at[side],
            device_id=neighbour(1),
            device_id_type=pl.DeviceIdType.MESH,
        ).wait_recv()

    def halo_sent():
        pl.when(jnp.logical_not(at_end))(lambda: halo_copy(1).wait_send())
        pl.when(jnp.logical_not(at_start))(lambda: halo_copy(0).wait_send())

    def standardise(values):
        average = jnp.mean(values, axis=-1, keepdims=True)
        centered = values - average
        variance = jnp.mean(centered * centered, axis=-1, keepdims=True)
        inverse = lax.rsqrt(variance + EPSILON)
        return centered * inverse, inverse

    few = 64

    def norm_rows(source, target, target_row, rows):
        def one(step, carry):
            values = source[pl.ds(pl.multiple_of(step * few, few), few), :].astype(f32)
            rounded = (standardise(values)[0] * gain[...]).astype(bf16)
            target[pl.ds(pl.multiple_of(target_row + step * few, few), few), :] = rounded
            return carry

        lax.fori_loop(0, rows // few, one, 0)

    def multiply_into(target, rows, left, weight, side):
        for start in range(0, channels, strip):
            cols = slice(start, start + strip)
            other = weight[:, cols] if side == 0 else weight[cols, :]
            target[rows, cols] = dot(left, other, ((1,), (side,))).astype(target.dtype)

    loads[0].wait()
    norm_rows(frames, normed, 0, length)
    own = slice(WINDOW, WINDOW + length)

    piece = min(128, tile_rows)

    def store_turned(target, first, cols, turned):
        for start in range(0, 128, piece):
            block = (first + start) // tile_rows
            down = (block // 2) * tile_rows + (first + start) % tile_rows
            target[block % 2, pl.ds(pl.multiple_of(down, piece), piece), cols] = turned[start : start + piece]

    def turn(source, row, place, rows):
        for start in range(0, rows, 128):
            for col in range(0, channels, 128):
                down = pl.ds(pl.multiple_of(row + start, 128), 128)
                cols = pl.ds(pl.multiple_of(place + start, 128), 128)
                tile = source[down, col : col + 128]
                store_turned(normed_t, col, cols, tile.astype(f32).T.astype(bf16))

    turn(normed, 0, WINDOW, length)
    send_far()
    weight_wait(3)
    loads[1].wait()
    everything = slice(0, length)
    multiply_into(upstream, everything, cotangent[...], w_out, 1)
    for which, target, rows in ((0, query, everything), (1, key, own), (2, value, own)):
        weight_wait(which)
        multiply_into(target, rows, normed[...], w_qkv.at[which], 0)

    def halo_rows(side):
        halo_wait(side)
        first = pl.multiple_of(side * WINDOW, WINDOW)
        start = pl.multiple_of(side * (length + WINDOW), WINDOW)
        norm_rows(halo.at[side], halo_normed, first, WINDOW)
        turn(halo_normed, first, start, WINDOW)

    def halo_project(side, cols):
        first = pl.multiple_of(side * WINDOW, WINDOW)
        start = pl.multiple_of(side * (length + WINDOW), WINDOW)
        for which, target in ((1, key), (2, value)):
            made = dot(halo_normed[pl.ds(first, WINDOW), :], w_qkv[which, :, cols], ((1,), (0,)))
            target[pl.ds(start, WINDOW), cols] = made.astype(bf16)

    def edge_copy(side):
        return pltpu.make_async_remote_copy(
            src_ref=edge_out.at[side],
            dst_ref=edge_in.at[side],
            send_sem=edge_send.at[side],
            recv_sem=edge_recv.at[side],
            device_id=neighbour(-1 if side == 0 else 1),
            device_id_type=pl.DeviceIdType.MESH,
        )

    blocks = length // WINDOW
    span = 3 * WINDOW
    score_scale = HEAD_SIZE ** (-0.5)
    row = lax.broadcasted_iota(jnp.int32, (WINDOW, span), 0)
    col = lax.broadcasted_iota(jnp.int32, (WINDOW, span), 1)
    near = (col >= row) & (col <= row + 2 * WINDOW)

    def head_of(pair, member):
        return 2 * pairs - 1 - pair if member else pair

    def attend(pair, block):
        for member in range(2):
            lane = pl.multiple_of(pair * wide + member * HEAD_SIZE, HEAD_SIZE)
            lanes = pl.ds(lane, HEAD_SIZE)
            real = head_of(pair, member) * HEAD_SIZE
            start = pl.multiple_of(block * WINDOW, WINDOW)
            rows, keys = pl.ds(start, WINDOW), pl.ds(start, span)
            q, k, v, up = query[rows, lanes], key[keys, lanes], value[keys, lanes], upstream[rows, lanes]
            frame = position * length + (block - 1) * WINDOW + col
            allowed = near & (frame >= 0) & (frame < devices * length)
            scores = jnp.where(allowed, dot(q, k, ((1,), (1,))) * score_scale, MASKED)
            share = jnp.exp(scores - jnp.max(scores, axis=-1, keepdims=True))
            rounded = (share * (1.0 / jnp.sum(share, axis=-1, keepdims=True))).astype(bf16)
            mixed = dot(rounded, v, ((1,), (0,)))
            attended[rows, lanes] = mixed.astype(bf16)
            store_turned(attended_t, real, rows, mixed.T.astype(bf16))
            share = rounded.astype(f32)
            grad = dot(up, v, ((1,), (1,)))
            centre = jnp.sum(share * grad, axis=-1, keepdims=True)
            grad = (share * (grad - centre) * score_scale).astype(bf16)
            grad_query[rows, lanes] = dot(grad, k, ((1,), (0,))).astype(bf16)
            grad_sum[0, keys, lanes] += dot(grad, q, ((0,), (0,)))
            grad_sum[1, keys, lanes] += dot(rounded, up, ((0,), (0,)))

    def near_step(pair, carry):
        cols = pl.ds(pl.multiple_of(pair * wide, wide), wide)
        grad_sum[:, :, cols] = jnp.zeros((2, length + 2 * WINDOW, wide), f32)
        halo_project(near_side, cols)
        for step in range(blocks - 1):
            attend(pair, near_side + step)
        return carry

    def spot(lane, block):
        return sum(((block >> bit) & 1) * (outer >> (step + 1)) for step, bit in enumerate(orders[lane]))

    def base(lane, stage):
        total = 0
        for step in range(stage):
            total = total + bit_at(orders[lane][step]) * (outer >> (step + 1))
        return total

    def landing(stage):
        return outer - (outer >> stage)

    def leaving(lane, stage):
        return base(lane, stage) + (1 - bit_at(orders[lane][stage])) * (outer >> (stage + 1))

    def remote(source, target, send, recv, device):
        return pltpu.make_async_remote_copy(
            src_ref=source,
            dst_ref=target,
            send_sem=send,
            recv_sem=recv,
            device_id=device,
            device_id_type=pl.DeviceIdType.MESH,
        )

    def core_copy(mail, got, chunk):
        return remote(mail, got, core_send.at[chunk], core_recv.at[chunk], other_core)

    def stage_copy(held, landed, chunk, lane, stage):
        half = outer >> (stage + 1)
        return remote(
            held.at[lane, pl.ds(leaving(lane, stage), half)],
            landed.at[lane, pl.ds(landing(stage), half)],
            stage_send.at[chunk, lane, stage],
            stage_recv.at[chunk, lane, stage],
            partner(orders[lane][stage]),
        )

    def gathered(bufs, lane, stage, where, *index):
        held, got, landed = bufs
        total = held[lane, where, *index].astype(f32) + got[lane, where, *index].astype(f32)
        for step in range(stage):
            place = landing(step) + where - base(lane, step + 1)
            total = total + landed[lane, place, *index].astype(f32)
        return total

    def reduce_stage(bufs, chunk, lane, stage, inner):
        held, got, landed = bufs
        half = outer >> (stage + 1)
        start = leaving(lane, stage)

        def add(step, carry):
            where, index = start + step // inner, step % inner
            held[lane, where, index] = gathered(bufs, lane, stage, where, index).astype(bf16)
            return carry

        lax.fori_loop(0, half * inner, add, 0)
        stage_copy(held, landed, chunk, lane, stage).start()

    def wait_stage(bufs, mail, chunk, lane, stage):
        held, got, landed = bufs
        if stage == 0:
            if lane == 0:
                core_copy(mail, got, chunk).wait()
        else:
            stage_copy(held, landed, chunk, lane, stage - 1).wait()

    def owner(pair, member):
        return head_of(pair, member) // heads_each

    def tile_copy(pair, lane, member, away):
        return remote(
            held.at[pair, lane, base(lane, levels), member],
            last.at[pair, lane, member, away - 1],
            last_send.at[pair, lane, member],
            last_recv.at[pair, lane, member, away - 1],
            (seq, owner(pair, member)),
        )

    def advance(pair, stage):
        bufs = held.at[pair], got.at[pair], landed.at[pair]
        for lane in range(2):
            wait_stage(bufs, mail.at[pair], pair, lane, stage)
            if stage < levels:
                reduce_stage(bufs, pair, lane, stage, 2)
                continue
            where = base(lane, levels)
            for member in range(2):
                held[pair, lane, where, member] = gathered(bufs, lane, stage, where, member).astype(bf16)

                @pl.when(owner(pair, member) != head)
                def _():
                    tile_copy(pair, lane, member, (head - owner(pair, member) + head_size) % head_size).start()

    def finish(pair):
        for member in range(2):
            mine = owner(pair, member) == head
            inside = (head_of(pair, member) % heads_each) * HEAD_SIZE

            @pl.when(mine)
            def _():
                for lane in range(2):
                    total = held[pair, lane, base(lane, levels), member].astype(f32)
                    for away in range(1, head_size):
                        tile_copy(pair, lane, member, away).wait_recv()
                        total = total + last[pair, lane, member, away - 1].astype(f32)
                    rows = slice(lane * part_rows, (lane + 1) * part_rows)
                    grad_qkv[:, rows, pl.ds(pl.multiple_of(inside, HEAD_SIZE), HEAD_SIZE)] = total

            @pl.when(jnp.logical_not(mine))
            def _():
                for lane in range(2):
                    tile_copy(pair, lane, member, 1).wait_send()

    def last_copy(lane, step):
        return remote(
            held_out.at[lane, base(lane, levels), (head + step) % head_size],
            last_out.at[lane, step - 1],
            last_send_out.at[lane, step - 1],
            last_recv_out.at[lane, step - 1],
            along(step),
        )

    def advance_out(stage):
        bufs = held_out, got_out, landed_out
        for lane in range(2):
            wait_stage(bufs, mail_out, pairs, lane, stage)
            if stage < levels:
                reduce_stage(bufs, pairs, lane, stage, head_size)
                continue
            where = base(lane, levels)
            for step in range(1, head_size):
                other = (head + step) % head_size
                held_out[lane, where, other] = gathered(bufs, lane, stage, where, other).astype(bf16)
                last_copy(lane, step).start()

    def finish_out():
        bufs = held_out, got_out, landed_out
        for lane in range(2):
            total = gathered(bufs, lane, levels, base(lane, levels), head)
            for step in range(1, head_size):
                last_copy(lane, step).wait()
                total = total + last_out[lane, step - 1].astype(f32)
            grad_out[lane * part_rows : (lane + 1) * part_rows, :] = total

    whole = slice(0, 2 * WINDOW + length)

    def products(pair, target, parity):
        cols = pl.ds(pl.multiple_of(pair * wide, wide), wide)
        for which in range(3):
            right = grad_query[:, cols] if which == 0 else grad_pair[which - 1, :, cols]
            product = dot(normed_t[parity, :, own if which == 0 else whole], right, ((1,), (0,))).astype(bf16)
            for block in range(outer):
                for lane in range(2):
                    start = block * tile_rows + lane * part_rows
                    for member in range(2):
                        target[pair, lane, spot(lane, block), member, which] = product[
                            start : start + part_rows, member * HEAD_SIZE : (member + 1) * HEAD_SIZE
                        ]

    def products_out(target, parity):
        def one(index, carry):
            cols = pl.ds(pl.multiple_of(index * tile_cols, tile_cols), tile_cols)
            product = dot(attended_t[parity], cotangent[:, cols], ((1,), (0,))).astype(bf16)
            for block in range(outer):
                for lane in range(2):
                    start = block * tile_rows + lane * part_rows
                    target[lane, spot(lane, block), index] = product[start : start + part_rows]
            return carry

        lax.fori_loop(0, head_size, one, 0)

    def pair_back(rows, cols):
        term = dot(grad_pair[0, rows, :], w_qkv[1, cols, :], ((1,), (1,)))
        return term + dot(grad_pair[1, rows, :], w_qkv[2, cols, :], ((1,), (1,)))

    def norm_back(step, carry):
        rows = pl.ds(pl.multiple_of(step * few, few), few)
        unit, inverse = standardise(frames[rows, :].astype(f32))
        grad = grad_normed[rows, :].astype(bf16).astype(f32) * gain[...]
        average = jnp.mean(grad, axis=-1, keepdims=True)
        along_unit = jnp.mean(grad * unit, axis=-1, keepdims=True)
        grad = inverse * (grad - average - unit * along_unit)
        grad_frames[rows, :] = (cotangent[rows, :].astype(f32) + grad).astype(bf16)
        return carry

    def send_edges():
        for side in range(2):
            start = side * (length + WINDOW)
            for strip_start in range(0, channels, strip):
                cols = slice(strip_start, strip_start + strip)
                edge_out[side, :, cols] = pair_back(slice(start, start + WINDOW), cols).astype(bf16)
            edge_copy(side).start()

    def far_step(pair):
        cols = pl.ds(pl.multiple_of(pair * wide, wide), wide)
        halo_project(1 - near_side, cols)
        attend(pair, (1 - near_side) * (blocks - 1))
        grad_pair[:, :, cols] = grad_sum[:, :, cols].astype(bf16)

    def pair_step(pair, carry):
        products(pair, mail, 1 - core)
        core_copy(mail.at[pair], got.at[pair], pair).start()
        products(pair, held, core)

        @pl.when(pair < pairs - 1)
        def _():
            far_step(pair + 1)

        @pl.when(pair == pairs - 1)
        def _():
            send_edges()

        for stage in range(levels + 1):

            @pl.when(pair >= stage)
            def _():
                advance(pair - stage, stage)

        @pl.when(pair == 1)
        def _():
            near_step(pairs - 1, 0)

        return carry

    halo_rows(near_side)
    lax.fori_loop(0, pairs - 1, near_step, 0)
    halo_rows(1 - near_side)
    halo_sent()
    far_step(0)
    lax.fori_loop(0, pairs, pair_step, 0)

    def drain(step):
        for stage in range(levels + 1):
            pair = pairs + step - stage
            if pair < pairs:
                advance(pair, stage)
            elif pair == pairs:
                advance_out(stage)

    products_out(mail_out, 1 - core)
    core_copy(mail_out, got_out, pairs).start()
    products_out(held_out, core)
    drain(0)
    drain(1)
    for start in range(0, channels, strip):
        cols = slice(start, start + strip)
        mixed = dot(attended[...], w_out[:, cols], ((1,), (0,)))
        output[:, cols] = (frames[:, cols].astype(f32) + mixed).astype(bf16)
    for start in range(0, channels, strip):
        cols = slice(start, start + strip)
        grad_normed[:, cols] = pair_back(own, cols) + dot(grad_query[...], w_qkv[0, cols, :], ((1,), (1,)))
    for step in range(2, levels + 1):
        drain(step)
    edge_copy(0).wait()
    edge_copy(1).wait()
    grad_normed[:WINDOW, :] += edge_in[1].astype(f32)
    grad_normed[length - WINDOW :, :] += edge_in[0].astype(f32)
    lax.fori_loop(0, length // few, norm_back, 0)

    def finish_pair(pair, carry):
        finish(pair)
        return carry

    lax.fori_loop(0, pairs, finish_pair, 0)
    finish_out()


def deliver_kernel(scale, output, grad_frames, grad_qkv, grad_out, *targets):
    targets[0][...] = output[...]
    targets[1][...] = grad_frames[...]
    targets[2][...] = grad_qkv[...] * scale
    targets[3][...] = grad_out[...] * scale


def shards(frames, cotangent, norm_gain, w_qkv, w_out):
    length, channels = frames.shape
    seq_size, head_size = lax.axis_size("seq"), lax.axis_size("head")
    devices = seq_size * head_size
    bordered = length + 2 * WINDOW
    tile_rows, tile_cols = channels // seq_size, channels // head_size
    outer, pairs = seq_size // 2, channels // (2 * HEAD_SIZE)
    levels = len(bits_of(outer))
    pair_part = (2, 3, tile_rows // 2, HEAD_SIZE)
    out_part = (tile_rows // 2, tile_cols)
    bf16, f32 = jnp.bfloat16, jnp.float32
    vmem, anywhere = pl.BlockSpec(memory_space=pltpu.VMEM), pl.BlockSpec(memory_space=pl.ANY)
    dma = pltpu.SemaphoreType.DMA
    shapes = [
        jax.ShapeDtypeStruct((length, channels), bf16),
        jax.ShapeDtypeStruct((length, channels), bf16),
        jax.ShapeDtypeStruct((3, tile_rows, tile_cols), f32),
        jax.ShapeDtypeStruct((tile_rows, tile_cols), f32),
    ]
    results = pl.pallas_call(
        functools.partial(block_kernel, (seq_size, head_size)),
        out_shape=[pltpu.VMEM(one.shape, one.dtype) for one in shapes],
        in_specs=[anywhere, anywhere, vmem, anywhere, anywhere],
        out_specs=[vmem] * 4,
        scratch_shapes=[
            pltpu.VMEM((length, channels), bf16),
            pltpu.VMEM((length, channels), bf16),
            pltpu.VMEM((3, channels, channels), bf16),
            pltpu.VMEM((channels, channels), bf16),
            pltpu.VMEM((length, channels), bf16),
            pltpu.VMEM((2, channels // 2, bordered), bf16),
            pltpu.VMEM((length, channels), bf16),
            pltpu.VMEM((bordered, channels), bf16),
            pltpu.VMEM((bordered, channels), bf16),
            pltpu.VMEM((length, channels), bf16),
            pltpu.VMEM((length, channels), bf16),
            pltpu.VMEM((2, channels // 2, length), bf16),
            pltpu.VMEM((length, channels), bf16),
            pltpu.VMEM((2, bordered, channels), bf16),
            pltpu.VMEM((2, bordered, channels), f32),
            pltpu.VMEM((2, WINDOW, channels), bf16),
            pltpu.VMEM((2, WINDOW, channels), bf16),
            pltpu.VMEM((length, channels), f32),
            pltpu.VMEM((2, WINDOW, channels), bf16),
            pltpu.VMEM((2 * WINDOW, channels), bf16),
            pltpu.VMEM((pairs, 2, outer, *pair_part), bf16),
            pltpu.VMEM((pairs, 2, outer, *pair_part), bf16),
            pltpu.VMEM((pairs, 2, outer, *pair_part), bf16),
            pltpu.VMEM((pairs, 2, outer - 1, *pair_part), bf16),
            pltpu.VMEM((pairs, 2, 2, head_size - 1, *pair_part[1:]), bf16),
            pltpu.VMEM((2, outer, head_size, *out_part), bf16),
            pltpu.VMEM((2, outer, head_size, *out_part), bf16),
            pltpu.VMEM((2, outer, head_size, *out_part), bf16),
            pltpu.VMEM((2, outer - 1, head_size, *out_part), bf16),
            pltpu.VMEM((2, head_size - 1, *out_part), bf16),
            dma((2,)),
            dma((4,)),
            dma((2,)),
            dma((2,)),
            dma((2,)),
            dma((2,)),
            dma((pairs + 1,)),
            dma((pairs + 1,)),
            dma((pairs + 1, 2, levels)),
            dma((pairs + 1, 2, levels)),
            dma((pairs, 2, 2)),
            dma((pairs, 2, 2, head_size - 1)),
            dma((2, head_size - 1)),
            dma((2, head_size - 1)),
        ],
        compiler_params=pltpu.CompilerParams(
            collective_id=0, has_side_effects=True, vmem_limit_bytes=60 * 2**20
        ),
        name="block",
    )(frames, cotangent, norm_gain.reshape(1, channels), w_qkv, w_out)
    return tuple(
        pl.pallas_call(
            functools.partial(deliver_kernel, (devices * length) ** (-0.5)),
            out_shape=shapes,
            in_specs=[vmem] * 4,
            out_specs=[vmem] * 4,
            name="deliver",
        )(*[pltpu.with_memory_space_constraint(one, pltpu.VMEM) for one in results])
    )


def solution(mesh):
    in_specs = (P(("seq", "head"), None), P(("seq", "head"), None), P(), P(), P())
    out_specs = (
        P(("seq", "head"), None),
        P(("seq", "head"), None),
        P(None, "seq", "head"),
        P("seq", "head"),
    )
    return jax.shard_map(shards, mesh=mesh, in_specs=in_specs, out_specs=out_specs, check_vma=False)
```

```python
import functools

import jax
import jax.numpy as jnp
from jax import lax
from jax.experimental import pallas as pl
from jax.experimental.pallas import tpu as pltpu
from jax.sharding import PartitionSpec as P

HEAD_SIZE = 128
WINDOW = 128

EPSILON = 1e-05
MASKED = -1e30
AXES = ("seq", "head")


def dot(a, b, contract):
    return lax.dot_general(a, b, (contract, ((), ())), preferred_element_type=jnp.float32)


def bits_of(size):
    return list(range(size.bit_length() - 1))


def block_kernel(
    sizes,
    frames_hbm, cotangent_hbm, gain, w_qkv_hbm, w_out_hbm,
    output, grad_frames, grad_qkv, grad_out,
    frames, cotangent, w_qkv, w_out, normed, normed_t, query, key, value, upstream, attended, attended_t,
    grad_query, grad_pair, grad_sum, edge_out, edge_in, grad_normed, halo, halo_normed,
    mail, got, held, landed, last, mail_out, got_out, held_out, landed_out, last_out,
    rows_sem, weight_sem, halo_send, halo_recv, edge_send, edge_recv,
    core_send, core_recv, stage_send, stage_recv, last_send, last_recv, last_send_out, last_recv_out,
):
    seq_size, head_size = sizes
    devices = seq_size * head_size
    length, channels = frames_hbm.shape
    outer, part_rows, tile_cols = held_out.shape[1], held_out.shape[3], held_out.shape[4]
    tile_rows = 2 * part_rows
    bits = bits_of(outer)
    orders = (bits, bits[::-1])
    levels = len(bits)
    seq, head = lax.axis_index("seq"), lax.axis_index("head")
    core, row_block = seq % 2, seq // 2
    position = seq * head_size + head
    bf16, f32 = jnp.bfloat16, jnp.float32
    strip = min(256, channels)

    def neighbour(step):
        there = (position + step + devices) % devices
        return (there // head_size, there % head_size)

    def bit_at(bit):
        return (row_block // 2**bit) % 2

    def partner(bit):
        return (2 * (row_block + (1 - 2 * bit_at(bit)) * 2**bit) + core, head)

    def along(step):
        return (seq, (head + step) % head_size)

    wide = 2 * HEAD_SIZE
    pairs = channels // wide
    heads_each = tile_cols // HEAD_SIZE

    loads = [
        pltpu.make_async_copy(frames_hbm, frames, rows_sem.at[0]),
        pltpu.make_async_copy(cotangent_hbm, cotangent, rows_sem.at[1]),
    ]
    loads[0].start()

    def weight_wait(which):
        if which == 3:
            pltpu.make_async_copy(w_out_hbm, w_out, weight_sem.at[3]).wait()
        else:
            pltpu.make_async_copy(w_qkv_hbm.at[which], w_qkv.at[which], weight_sem.at[which]).wait()

    other_core = (2 * row_block + 1 - core, head)
    greeted = [other_core] + [partner(bit) for bit in bits]
    greeted += [along(step) for step in range(1, head_size)] + [neighbour(1), neighbour(-1)]
    barrier = pltpu.get_barrier_semaphore()
    for device in greeted:
        pl.semaphore_signal(barrier, inc=1, device_id=device, device_id_type=pl.DeviceIdType.MESH)
    pl.semaphore_wait(barrier, len(greeted))

    def halo_copy(side):
        rows = pl.ds(length - WINDOW, WINDOW) if side == 0 else pl.ds(0, WINDOW)
        return pltpu.make_async_remote_copy(
            src_ref=frames_hbm.at[rows],
            dst_ref=halo.at[side],
            send_sem=halo_send.at[side],
            recv_sem=halo_recv.at[side],
            device_id=neighbour(1 if side == 0 else -1),
            device_id_type=pl.DeviceIdType.MESH,
        )

    at_start, at_end = head == 0, head == head_size - 1
    pl.when(jnp.logical_not(at_end))(lambda: halo_copy(0).start())
    pl.when(jnp.logical_not(at_start))(lambda: halo_copy(1).start())
    near_side = (head == 0).astype(jnp.int32)
    loads[1].start()

    for slot in range(2 * pairs):
        real = (2 * pairs - 1 - slot // 2) if slot % 2 else slot // 2
        there, here = pl.ds(real * HEAD_SIZE, HEAD_SIZE), pl.ds(slot * HEAD_SIZE, HEAD_SIZE)
        pltpu.make_async_copy(w_out_hbm.at[there], w_out.at[here], weight_sem.at[3]).start()
    for which in range(3):
        for slot in range(2 * pairs):
            real = (2 * pairs - 1 - slot // 2) if slot % 2 else slot // 2
            there, here = pl.ds(real * HEAD_SIZE, HEAD_SIZE), pl.ds(slot * HEAD_SIZE, HEAD_SIZE)
            pltpu.make_async_copy(
                w_qkv_hbm.at[which, :, there], w_qkv.at[which, :, here], weight_sem.at[which]
            ).start()


    def send_far():
        @pl.when(at_end)
        def _():
            halo_copy(1).wait_send()
            halo_copy(0).start()

        @pl.when(at_start)
        def _():
            halo_copy(0).wait_send()
            halo_copy(1).start()

    def halo_wait(side):
        pltpu.make_async_remote_copy(
            src_ref=frames_hbm.at[pl.ds(0, WINDOW)],
            dst_ref=halo.at[side],
            send_sem=halo_send.at[side],
            recv_sem=halo_recv.at[side],
            device_id=neighbour(1),
            device_id_type=pl.DeviceIdType.MESH,
        ).wait_recv()

    def halo_sent():
        pl.when(jnp.logical_not(at_end))(lambda: halo_copy(1).wait_send())
        pl.when(jnp.logical_not(at_start))(lambda: halo_copy(0).wait_send())

    def standardise(values):
        average = jnp.mean(values, axis=-1, keepdims=True)
        centered = values - average
        variance = jnp.mean(centered * centered, axis=-1, keepdims=True)
        inverse = lax.rsqrt(variance + EPSILON)
        return centered * inverse, inverse

    few = 64

    def norm_rows(source, target, target_row, rows):
        def one(step, carry):
            values = source[pl.ds(pl.multiple_of(step * few, few), few), :].astype(f32)
            rounded = (standardise(values)[0] * gain[...]).astype(bf16)
            target[pl.ds(pl.multiple_of(target_row + step * few, few), few), :] = rounded
            return carry

        lax.fori_loop(0, rows // few, one, 0)

    def multiply_into(target, rows, left, weight, side):
        for start in range(0, channels, strip):
            cols = slice(start, start + strip)
            other = weight[:, cols] if side == 0 else weight[cols, :]
            target[rows, cols] = dot(left, other, ((1,), (side,))).astype(target.dtype)

    loads[0].wait()
    norm_rows(frames, normed, 0, length)
    own = slice(WINDOW, WINDOW + length)

    piece = min(128, tile_rows)

    def store_turned(target, first, cols, turned):
        for start in range(0, 128, piece):
            block = (first + start) // tile_rows
            down = (block // 2) * tile_rows + (first + start) % tile_rows
            target[block % 2, pl.ds(pl.multiple_of(down, piece), piece), cols] = turned[start : start + piece]

    def turn(source, row, place, rows):
        for start in range(0, rows, 128):
            for col in range(0, channels, 128):
                down = pl.ds(pl.multiple_of(row + start, 128), 128)
                cols = pl.ds(pl.multiple_of(place + start, 128), 128)
                tile = source[down, col : col + 128]
                store_turned(normed_t, col, cols, tile.astype(f32).T.astype(bf16))

    turn(normed, 0, WINDOW, length)
    send_far()
    weight_wait(3)
    loads[1].wait()
    everything = slice(0, length)
    multiply_into(upstream, everything, cotangent[...], w_out, 1)
    for which, target, rows in ((0, query, everything), (1, key, own), (2, value, own)):
        weight_wait(which)
        multiply_into(target, rows, normed[...], w_qkv.at[which], 0)

    def halo_rows(side):
        halo_wait(side)
        first = pl.multiple_of(side * WINDOW, WINDOW)
        start = pl.multiple_of(side * (length + WINDOW), WINDOW)
        norm_rows(halo.at[side], halo_normed, first, WINDOW)
        turn(halo_normed, first, start, WINDOW)

    def halo_project(side, cols):
        first = pl.multiple_of(side * WINDOW, WINDOW)
        start = pl.multiple_of(side * (length + WINDOW), WINDOW)
        for which, target in ((1, key), (2, value)):
            made = dot(halo_normed[pl.ds(first, WINDOW), :], w_qkv[which, :, cols], ((1,), (0,)))
            target[pl.ds(start, WINDOW), cols] = made.astype(bf16)

    def edge_copy(side):
        return pltpu.make_async_remote_copy(
            src_ref=edge_out.at[side],
            dst_ref=edge_in.at[side],
            send_sem=edge_send.at[side],
            recv_sem=edge_recv.at[side],
            device_id=neighbour(-1 if side == 0 else 1),
            device_id_type=pl.DeviceIdType.MESH,
        )

    blocks = length // WINDOW
    span = 3 * WINDOW
    score_scale = HEAD_SIZE ** (-0.5)
    row = lax.broadcasted_iota(jnp.int32, (WINDOW, span), 0)
    col = lax.broadcasted_iota(jnp.int32, (WINDOW, span), 1)
    near = (col >= row) & (col <= row + 2 * WINDOW)

    def head_of(pair, member):
        return 2 * pairs - 1 - pair if member else pair

    def attend(pair, block):
        for member in range(2):
            lane = pl.multiple_of(pair * wide + member * HEAD_SIZE, HEAD_SIZE)
            lanes = pl.ds(lane, HEAD_SIZE)
            real = head_of(pair, member) * HEAD_SIZE
            start = pl.multiple_of(block * WINDOW, WINDOW)
            rows, keys = pl.ds(start, WINDOW), pl.ds(start, span)
            q, k, v, up = query[rows, lanes], key[keys, lanes], value[keys, lanes], upstream[rows, lanes]
            frame = position * length + (block - 1) * WINDOW + col
            allowed = near & (frame >= 0) & (frame < devices * length)
            scores = jnp.where(allowed, dot(q, k, ((1,), (1,))) * score_scale, MASKED)
            share = jnp.exp(scores - jnp.max(scores, axis=-1, keepdims=True))
            rounded = (share * (1.0 / jnp.sum(share, axis=-1, keepdims=True))).astype(bf16)
            mixed = dot(rounded, v, ((1,), (0,)))
            attended[rows, lanes] = mixed.astype(bf16)
            store_turned(attended_t, real, rows, mixed.T.astype(bf16))
            share = rounded.astype(f32)
            grad = dot(up, v, ((1,), (1,)))
            centre = jnp.sum(share * grad, axis=-1, keepdims=True)
            grad = (share * (grad - centre) * score_scale).astype(bf16)
            grad_query[rows, lanes] = dot(grad, k, ((1,), (0,))).astype(bf16)
            grad_sum[0, keys, lanes] += dot(grad, q, ((0,), (0,)))
            grad_sum[1, keys, lanes] += dot(rounded, up, ((0,), (0,)))

    def near_step(pair, carry):
        cols = pl.ds(pl.multiple_of(pair * wide, wide), wide)
        grad_sum[:, :, cols] = jnp.zeros((2, length + 2 * WINDOW, wide), f32)
        halo_project(near_side, cols)
        for step in range(blocks - 1):
            attend(pair, near_side + step)
        return carry

    def spot(lane, block):
        return sum(((block >> bit) & 1) * (outer >> (step + 1)) for step, bit in enumerate(orders[lane]))

    def base(lane, stage):
        total = 0
        for step in range(stage):
            total = total + bit_at(orders[lane][step]) * (outer >> (step + 1))
        return total

    def landing(stage):
        return outer - (outer >> stage)

    def leaving(lane, stage):
        return base(lane, stage) + (1 - bit_at(orders[lane][stage])) * (outer >> (stage + 1))

    def remote(source, target, send, recv, device):
        return pltpu.make_async_remote_copy(
            src_ref=source,
            dst_ref=target,
            send_sem=send,
            recv_sem=recv,
            device_id=device,
            device_id_type=pl.DeviceIdType.MESH,
        )

    def core_copy(mail, got, chunk):
        return remote(mail, got, core_send.at[chunk], core_recv.at[chunk], other_core)

    def stage_copy(held, landed, chunk, lane, stage):
        half = outer >> (stage + 1)
        return remote(
            held.at[lane, pl.ds(leaving(lane, stage), half)],
            landed.at[lane, pl.ds(landing(stage), half)],
            stage_send.at[chunk, lane, stage],
            stage_recv.at[chunk, lane, stage],
            partner(orders[lane][stage]),
        )

    def gathered(bufs, lane, stage, where, *index):
        held, got, landed = bufs
        total = held[lane, where, *index].astype(f32) + got[lane, where, *index].astype(f32)
        for step in range(stage):
            place = landing(step) + where - base(lane, step + 1)
            total = total + landed[lane, place, *index].astype(f32)
        return total

    def reduce_stage(bufs, chunk, lane, stage, inner):
        held, got, landed = bufs
        half = outer >> (stage + 1)
        start = leaving(lane, stage)

        def add(step, carry):
            where, index = start + step // inner, step % inner
            held[lane, where, index] = gathered(bufs, lane, stage, where, index).astype(bf16)
            return carry

        lax.fori_loop(0, half * inner, add, 0)
        stage_copy(held, landed, chunk, lane, stage).start()

    def wait_stage(bufs, mail, chunk, lane, stage):
        held, got, landed = bufs
        if stage == 0:
            if lane == 0:
                core_copy(mail, got, chunk).wait()
        else:
            stage_copy(held, landed, chunk, lane, stage - 1).wait()

    def owner(pair, member):
        return head_of(pair, member) // heads_each

    def tile_copy(pair, lane, member, away):
        return remote(
            held.at[pair, lane, base(lane, levels), member],
            last.at[pair, lane, member, away - 1],
            last_send.at[pair, lane, member],
            last_recv.at[pair, lane, member, away - 1],
            (seq, owner(pair, member)),
        )

    def advance(pair, stage):
        bufs = held.at[pair], got.at[pair], landed.at[pair]
        for lane in range(2):
            wait_stage(bufs, mail.at[pair], pair, lane, stage)
            if stage < levels:
                reduce_stage(bufs, pair, lane, stage, 2)
                continue
            where = base(lane, levels)
            for member in range(2):
                held[pair, lane, where, member] = gathered(bufs, lane, stage, where, member).astype(bf16)

                @pl.when(owner(pair, member) != head)
                def _():
                    tile_copy(pair, lane, member, (head - owner(pair, member) + head_size) % head_size).start()

    def finish(pair):
        for member in range(2):
            mine = owner(pair, member) == head
            inside = (head_of(pair, member) % heads_each) * HEAD_SIZE

            @pl.when(mine)
            def _():
                for lane in range(2):
                    total = held[pair, lane, base(lane, levels), member].astype(f32)
                    for away in range(1, head_size):
                        tile_copy(pair, lane, member, away).wait_recv()
                        total = total + last[pair, lane, member, away - 1].astype(f32)
                    rows = slice(lane * part_rows, (lane + 1) * part_rows)
                    grad_qkv[:, rows, pl.ds(pl.multiple_of(inside, HEAD_SIZE), HEAD_SIZE)] = total

            @pl.when(jnp.logical_not(mine))
            def _():
                for lane in range(2):
                    tile_copy(pair, lane, member, 1).wait_send()

    def last_copy(lane, step):
        return remote(
            held_out.at[lane, base(lane, levels), (head + step) % head_size],
            last_out.at[lane, step - 1],
            last_send_out.at[lane, step - 1],
            last_recv_out.at[lane, step - 1],
            along(step),
        )

    def advance_out(stage):
        bufs = held_out, got_out, landed_out
        for lane in range(2):
            wait_stage(bufs, mail_out, pairs, lane, stage)
            if stage < levels:
                reduce_stage(bufs, pairs, lane, stage, head_size)
                continue
            where = base(lane, levels)
            for step in range(1, head_size):
                other = (head + step) % head_size
                held_out[lane, where, other] = gathered(bufs, lane, stage, where, other).astype(bf16)
                last_copy(lane, step).start()

    def finish_out():
        bufs = held_out, got_out, landed_out
        for lane in range(2):
            total = gathered(bufs, lane, levels, base(lane, levels), head)
            for step in range(1, head_size):
                last_copy(lane, step).wait()
                total = total + last_out[lane, step - 1].astype(f32)
            grad_out[lane * part_rows : (lane + 1) * part_rows, :] = total

    whole = slice(0, 2 * WINDOW + length)

    def products(pair, target, parity):
        cols = pl.ds(pl.multiple_of(pair * wide, wide), wide)
        for which in range(3):
            right = grad_query[:, cols] if which == 0 else grad_pair[which - 1, :, cols]
            product = dot(normed_t[parity, :, own if which == 0 else whole], right, ((1,), (0,))).astype(bf16)
            for block in range(outer):
                for lane in range(2):
                    start = block * tile_rows + lane * part_rows
                    for member in range(2):
                        target[pair, lane, spot(lane, block), member, which] = product[
                            start : start + part_rows, member * HEAD_SIZE : (member + 1) * HEAD_SIZE
                        ]

    def products_out(target, parity):
        def one(index, carry):
            cols = pl.ds(pl.multiple_of(index * tile_cols, tile_cols), tile_cols)
            product = dot(attended_t[parity], cotangent[:, cols], ((1,), (0,))).astype(bf16)
            for block in range(outer):
                for lane in range(2):
                    start = block * tile_rows + lane * part_rows
                    target[lane, spot(lane, block), index] = product[start : start + part_rows]
            return carry

        lax.fori_loop(0, head_size, one, 0)

    def pair_back(rows, cols):
        term = dot(grad_pair[0, rows, :], w_qkv[1, cols, :], ((1,), (1,)))
        return term + dot(grad_pair[1, rows, :], w_qkv[2, cols, :], ((1,), (1,)))

    def norm_back(step, carry):
        rows = pl.ds(pl.multiple_of(step * few, few), few)
        unit, inverse = standardise(frames[rows, :].astype(f32))
        grad = grad_normed[rows, :].astype(bf16).astype(f32) * gain[...]
        average = jnp.mean(grad, axis=-1, keepdims=True)
        along_unit = jnp.mean(grad * unit, axis=-1, keepdims=True)
        grad = inverse * (grad - average - unit * along_unit)
        grad_frames[rows, :] = (cotangent[rows, :].astype(f32) + grad).astype(bf16)
        return carry

    def send_edges():
        def both(which):
            return jnp.concatenate([grad_pair[which, :WINDOW, :], grad_pair[which, WINDOW + length :, :]], axis=0)

        key_rows, value_rows = both(0), both(1)
        for start in range(0, channels, strip):
            cols = slice(start, start + strip)
            made = dot(key_rows, w_qkv[1, cols, :], ((1,), (1,))) + dot(value_rows, w_qkv[2, cols, :], ((1,), (1,)))
            made = made.astype(bf16)
            edge_out[0, :, cols] = made[:WINDOW]
            edge_out[1, :, cols] = made[WINDOW:]
        for side in range(2):
            edge_copy(side).start()

    def far_step(pair):
        cols = pl.ds(pl.multiple_of(pair * wide, wide), wide)
        halo_project(1 - near_side, cols)
        attend(pair, (1 - near_side) * (blocks - 1))
        grad_pair[:, :, cols] = grad_sum[:, :, cols].astype(bf16)

    def pair_step(pair, carry):
        products(pair, mail, 1 - core)
        core_copy(mail.at[pair], got.at[pair], pair).start()
        products(pair, held, core)

        @pl.when(pair < pairs - 1)
        def _():
            far_step(pair + 1)

        @pl.when(pair == pairs - 1)
        def _():
            send_edges()

        for stage in range(levels + 1):

            @pl.when(pair >= stage)
            def _():
                advance(pair - stage, stage)

        @pl.when(pair == 1)
        def _():
            near_step(pairs - 1, 0)

        return carry

    halo_rows(near_side)
    lax.fori_loop(0, pairs - 1, near_step, 0)
    halo_rows(1 - near_side)
    halo_sent()
    far_step(0)
    lax.fori_loop(0, pairs, pair_step, 0)

    def drain(step):
        for stage in range(levels + 1):
            pair = pairs + step - stage
            if pair < pairs:
                advance(pair, stage)
            elif pair == pairs:
                advance_out(stage)

    products_out(mail_out, 1 - core)
    core_copy(mail_out, got_out, pairs).start()
    products_out(held_out, core)
    drain(0)
    drain(1)
    for start in range(0, channels, strip):
        cols = slice(start, start + strip)
        mixed = dot(attended[...], w_out[:, cols], ((1,), (0,)))
        output[:, cols] = (frames[:, cols].astype(f32) + mixed).astype(bf16)
    for start in range(0, channels, strip):
        cols = slice(start, start + strip)
        grad_normed[:, cols] = pair_back(own, cols) + dot(grad_query[...], w_qkv[0, cols, :], ((1,), (1,)))
    for step in range(2, levels + 1):
        drain(step)
    edge_copy(0).wait()
    edge_copy(1).wait()
    grad_normed[:WINDOW, :] += edge_in[1].astype(f32)
    grad_normed[length - WINDOW :, :] += edge_in[0].astype(f32)
    lax.fori_loop(0, length // few, norm_back, 0)

    def finish_pair(pair, carry):
        finish(pair)
        return carry

    lax.fori_loop(0, pairs, finish_pair, 0)
    finish_out()


def deliver_kernel(scale, output, grad_frames, grad_qkv, grad_out, *targets):
    targets[0][...] = output[...]
    targets[1][...] = grad_frames[...]
    targets[2][...] = grad_qkv[...] * scale
    targets[3][...] = grad_out[...] * scale


def shards(frames, cotangent, norm_gain, w_qkv, w_out):
    length, channels = frames.shape
    seq_size, head_size = lax.axis_size("seq"), lax.axis_size("head")
    devices = seq_size * head_size
    bordered = length + 2 * WINDOW
    tile_rows, tile_cols = channels // seq_size, channels // head_size
    outer, pairs = seq_size // 2, channels // (2 * HEAD_SIZE)
    levels = len(bits_of(outer))
    pair_part = (2, 3, tile_rows // 2, HEAD_SIZE)
    out_part = (tile_rows // 2, tile_cols)
    bf16, f32 = jnp.bfloat16, jnp.float32
    vmem, anywhere = pl.BlockSpec(memory_space=pltpu.VMEM), pl.BlockSpec(memory_space=pl.ANY)
    dma = pltpu.SemaphoreType.DMA
    shapes = [
        jax.ShapeDtypeStruct((length, channels), bf16),
        jax.ShapeDtypeStruct((length, channels), bf16),
        jax.ShapeDtypeStruct((3, tile_rows, tile_cols), f32),
        jax.ShapeDtypeStruct((tile_rows, tile_cols), f32),
    ]
    results = pl.pallas_call(
        functools.partial(block_kernel, (seq_size, head_size)),
        out_shape=[pltpu.VMEM(one.shape, one.dtype) for one in shapes],
        in_specs=[anywhere, anywhere, vmem, anywhere, anywhere],
        out_specs=[vmem] * 4,
        scratch_shapes=[
            pltpu.VMEM((length, channels), bf16),
            pltpu.VMEM((length, channels), bf16),
            pltpu.VMEM((3, channels, channels), bf16),
            pltpu.VMEM((channels, channels), bf16),
            pltpu.VMEM((length, channels), bf16),
            pltpu.VMEM((2, channels // 2, bordered), bf16),
            pltpu.VMEM((length, channels), bf16),
            pltpu.VMEM((bordered, channels), bf16),
            pltpu.VMEM((bordered, channels), bf16),
            pltpu.VMEM((length, channels), bf16),
            pltpu.VMEM((length, channels), bf16),
            pltpu.VMEM((2, channels // 2, length), bf16),
            pltpu.VMEM((length, channels), bf16),
            pltpu.VMEM((2, bordered, channels), bf16),
            pltpu.VMEM((2, bordered, channels), f32),
            pltpu.VMEM((2, WINDOW, channels), bf16),
            pltpu.VMEM((2, WINDOW, channels), bf16),
            pltpu.VMEM((length, channels), f32),
            pltpu.VMEM((2, WINDOW, channels), bf16),
            pltpu.VMEM((2 * WINDOW, channels), bf16),
            pltpu.VMEM((pairs, 2, outer, *pair_part), bf16),
            pltpu.VMEM((pairs, 2, outer, *pair_part), bf16),
            pltpu.VMEM((pairs, 2, outer, *pair_part), bf16),
            pltpu.VMEM((pairs, 2, outer - 1, *pair_part), bf16),
            pltpu.VMEM((pairs, 2, 2, head_size - 1, *pair_part[1:]), bf16),
            pltpu.VMEM((2, outer, head_size, *out_part), bf16),
            pltpu.VMEM((2, outer, head_size, *out_part), bf16),
            pltpu.VMEM((2, outer, head_size, *out_part), bf16),
            pltpu.VMEM((2, outer - 1, head_size, *out_part), bf16),
            pltpu.VMEM((2, head_size - 1, *out_part), bf16),
            dma((2,)),
            dma((4,)),
            dma((2,)),
            dma((2,)),
            dma((2,)),
            dma((2,)),
            dma((pairs + 1,)),
            dma((pairs + 1,)),
            dma((pairs + 1, 2, levels)),
            dma((pairs + 1, 2, levels)),
            dma((pairs, 2, 2)),
            dma((pairs, 2, 2, head_size - 1)),
            dma((2, head_size - 1)),
            dma((2, head_size - 1)),
        ],
        compiler_params=pltpu.CompilerParams(
            collective_id=0, has_side_effects=True, vmem_limit_bytes=60 * 2**20
        ),
        name="block",
    )(frames, cotangent, norm_gain.reshape(1, channels), w_qkv, w_out)
    return tuple(
        pl.pallas_call(
            functools.partial(deliver_kernel, (devices * length) ** (-0.5)),
            out_shape=shapes,
            in_specs=[vmem] * 4,
            out_specs=[vmem] * 4,
            name="deliver",
        )(*[pltpu.with_memory_space_constraint(one, pltpu.VMEM) for one in results])
    )


def solution(mesh):
    in_specs = (P(("seq", "head"), None), P(("seq", "head"), None), P(), P(), P())
    out_specs = (
        P(("seq", "head"), None),
        P(("seq", "head"), None),
        P(None, "seq", "head"),
        P("seq", "head"),
    )
    return jax.shard_map(shards, mesh=mesh, in_specs=in_specs, out_specs=out_specs, check_vma=False)
```
